32 devices in a mesh: coil: 4 (over y, x), slab: 8 (over z, core).
Axes of the slice: x: 2, y: 2, z: 4, core: 2. Of those that a mesh axis runs over, the one named last changes fastest.
Arguments:
- coil_maps: float32 [8, 2, 8, 256, 128], P('coil', None, 'slab'), may hold values from -1.5 to 1.5
- kspace: float32 [8, 2, 8, 256, 128], P('coil', None, 'slab'), may hold values from -6 to 6
- sample_mask: int32 [256, 128], replicated, may hold values 0 or 1
- iterate: float32 [2, 8, 256, 128], P(None, 'slab', 'coil'), may hold values from -6 to 6
- probe_bits: int32 [2, 8, 256, 128], P(None, 'slab', 'coil'), may hold values from 0 to 1
- loss_gradient: float32 [2, 8, 256, 128], P(None, 'slab', 'coil'), may hold values from -6 to 6
- adjoint: float32 [2, 8, 256, 128], P(None, 'slab', 'coil'), may hold values from -6 to 6
- kernel_first: bfloat16 [24, 2, 3, 3, 3], replicated, may hold values from -0.875 to 0.875
- kernel_second: bfloat16 [24, 24, 3, 3, 3], replicated, may hold values from -0.25 to 0.25
- kernel_last: bfloat16 [2, 24, 3, 3, 3], replicated, may hold values from -0.25 to 0.25
Outputs:
- new_iterate: float32 [2, 8, 256, 128], P(None, 'slab', 'coil')
- probe_pullback: float32 [2, 8, 256, 128], P(None, 'slab', 'coil')
- adjoint_next: float32 [2, 8, 256, 128], P(None, 'slab', 'coil')
The draws below stay inside these ranges and needn't reach their ends.
Inputs may be any that keep to these rules, and one draw needn't show every extreme that they name: `sample_mask`: 1 marks a sampled phase-encode line. `probe_bits`: the probe's sign is 2 p - 1.
All inputs are finite; a program needn't handle non-finite values.
Results may differ from the reference program's by a relative error of at most 0.0055.
Values may be sent and summed in bfloat16 or wider, within the bound.
A program may use at most 128 MiB of HBM per device.

```python
import jax
import jax.numpy as jnp
from jax import lax

NC = 8
NY = 256
NZ = 128
CH = 24
NX = 8


def with_ends(entries, own_key, least, largest):
    shape = entries.shape
    place = [jax.random.randint(jax.random.fold_in(own_key, axis), (), 0, shape[axis]) for axis in range(len(shape))]
    entries = entries.at[tuple(place)].set(least)
    longest = shape.index(max(shape))
    place[longest] = (place[longest] + 1) % shape[longest]
    return entries.at[tuple(place)].set(largest)


def shard_levels(key, shape, pieces, low, high):
    factor_of = 1.0
    for axis_at, parts in pieces:
        heights = jax.random.uniform(jax.random.fold_in(jax.random.fold_in(key, 6), axis_at), (parts,), jnp.float32, low / len(pieces), high / len(pieces))
        factor_of = factor_of * jnp.repeat(jnp.exp(heights), shape[axis_at] // parts).reshape((-1,) + (1,) * (len(shape) - 1 - axis_at))
    return factor_of


def normal_values(stream_key, dims, deviation, bound, pieces=(), kind=jnp.bfloat16):
    values = deviation * jax.random.normal(stream_key, dims, jnp.float32)
    if pieces:
        values = values * shard_levels(stream_key, dims, pieces, -0.22, 0.18)
    return jnp.clip(values, -bound, bound).astype(kind)


def setup_inputs(seed: int = 0) -> dict:
    arg_keys = jax.random.split(jax.random.key(seed), 11)
    coil_maps = normal_values(arg_keys[0], (NC, 2, NX, NY, NZ), (2 * NC) ** -0.5, 1.5, ((0, 4), (2, 8)), jnp.float32)
    kspace = normal_values(arg_keys[1], (NC, 2, NX, NY, NZ), 1.0, 6.0, ((0, 4), (2, 8)), jnp.float32)
    sample_mask = with_ends((jax.random.randint(arg_keys[2], (NY, NZ), 0, 3) < 1).astype(jnp.int32), jax.random.fold_in(arg_keys[2], 1), 0, 1)
    iterate = normal_values(arg_keys[3], (2, NX, NY, NZ), 1.0, 6.0, ((1, 8), (2, 4)), jnp.float32)
    probe_bits = with_ends(jax.random.randint(arg_keys[4], (2, NX, NY, NZ), 0, 2), jax.random.fold_in(arg_keys[4], 1), 0, 1).astype(jnp.int32)
    loss_gradient = normal_values(arg_keys[5], (2, NX, NY, NZ), 1.0, 6.0, ((1, 8), (2, 4)), jnp.float32)
    adjoint = normal_values(arg_keys[6], (2, NX, NY, NZ), 1.0, 6.0, ((1, 8), (2, 4)), jnp.float32)
    kernel_first = normal_values(arg_keys[7], (CH, 2, 3, 3, 3), 54 ** -0.5, 0.875)
    kernel_second = normal_values(arg_keys[8], (CH, CH, 3, 3, 3), (27 * CH) ** -0.5, 0.25)
    kernel_last = normal_values(arg_keys[9], (2, CH, 3, 3, 3), (27 * CH) ** -0.5, 0.25)
    return {"coil_maps": coil_maps, "kspace": kspace, "sample_mask": sample_mask, "iterate": iterate, "probe_bits": probe_bits, "loss_gradient": loss_gradient, "adjoint": adjoint, "kernel_first": kernel_first, "kernel_second": kernel_second, "kernel_last": kernel_last}


step_size = 0.8
kernel_layout = ("NCDHW", "OIDHW", "NCDHW")


def spectrum(real_part, imag_part, inverse):
    joined = lax.complex(real_part, imag_part)
    if inverse:
        turned = jnp.fft.ifft2(joined, axes=(-2, -1), norm="ortho")
    else:
        turned = jnp.fft.fft2(joined, axes=(-2, -1), norm="ortho")
    return jnp.real(turned), jnp.imag(turned)


def coil_term(field, coil_map, mask_weight, data):
    field_real = field[:, 0]
    field_imag = field[:, 1]
    map_real = coil_map[0]
    map_imag = coil_map[1]
    coil_real = map_real * field_real - map_imag * field_imag
    coil_imag = map_real * field_imag + map_imag * field_real
    freq_real, freq_imag = spectrum(coil_real, coil_imag, False)
    freq_real = mask_weight * freq_real
    freq_imag = mask_weight * freq_imag
    if data is not None:
        freq_real = freq_real - mask_weight * data[0]
        freq_imag = freq_imag - mask_weight * data[1]
    back_real, back_imag = spectrum(freq_real, freq_imag, True)
    return jnp.stack([map_real * back_real + map_imag * back_imag,
                      map_real * back_imag - map_imag * back_real], axis=1)


def normal_sum(field, coil_maps, kspace, mask_weight, with_data):
    def coil_step(running, coil_index):
        data = kspace[coil_index] if with_data else None
        return running + coil_term(field, coil_maps[coil_index], mask_weight, data), None

    running, unused = lax.scan(coil_step, jnp.zeros(field.shape, jnp.float32),
                               jnp.arange(NC, dtype=jnp.int32))
    return running


def convolve(activation, kernel):
    return lax.conv_general_dilated(activation, kernel, (1, 1, 1), "SAME",
                                    dimension_numbers=kernel_layout,
                                    preferred_element_type=jnp.float32)


def transposed(kernel):
    return jnp.swapaxes(jnp.flip(kernel, (2, 3, 4)), 0, 1)


def silu_slope(preact):
    sigmoid_value = jax.nn.sigmoid(preact)
    return sigmoid_value * (1.0 + preact * (1.0 - sigmoid_value))


def reference(coil_maps, kspace, sample_mask, iterate, probe_bits, loss_gradient, adjoint,
              kernel_first, kernel_second, kernel_last):
    mask_weight = sample_mask.astype(jnp.float32)
    gradient = normal_sum(iterate[None], coil_maps, kspace, mask_weight, True)[0]
    relaxed = iterate - step_size * gradient
    activation = relaxed.astype(jnp.bfloat16)[None]
    preacts = []
    for kernel in (kernel_first, kernel_second):
        preact = convolve(activation, kernel)
        preacts.append(preact)
        activation = jax.nn.silu(preact).astype(jnp.bfloat16)
    new_iterate = relaxed + convolve(activation, kernel_last)[0]

    def pullback(cotangent):
        grad_field = convolve(cotangent.astype(jnp.bfloat16)[None], transposed(kernel_last))
        for kernel, preact in ((kernel_second, preacts[1]), (kernel_first, preacts[0])):
            grad_field = (grad_field * silu_slope(preact)).astype(jnp.bfloat16)
            grad_field = convolve(grad_field, transposed(kernel))
        return cotangent + grad_field[0]

    sign_field = (2 * probe_bits - 1).astype(jnp.float32)
    pulled = jnp.stack([pullback(sign_field), pullback(adjoint)])
    result = pulled - step_size * normal_sum(pulled, coil_maps, kspace, mask_weight, False)
    return new_iterate, result[0], loss_gradient + result[1]
```

```python
import jax
import jax.numpy as jnp
import numpy as np
from jax import lax
from jax.experimental import pallas as pl
from jax.experimental.pallas import tpu as pltpu
from jax.sharding import PartitionSpec as P

step_size = 0.8
reach = 4
f32 = jnp.float32
bf16 = jnp.bfloat16
in_hbm = pl.BlockSpec(memory_space=pltpu.HBM)
anywhere = pl.BlockSpec(memory_space=pl.ANY)
MESH = pl.DeviceIdType.MESH


class Channel:
    def __init__(self, axis, how, source, target, send_sem, recv_sem):
        self.axis, self.how, self.source, self.target = axis, how, source, target
        self.send_sem, self.recv_sem = send_sem, recv_sem
        self.size, self.mine = lax.axis_size(axis), lax.axis_index(axis)

    def row(self, rank):
        return self.source if self.how == "all" else self.source.at[rank]

    def copy(self, source_rank, target_row, device_rank, step):
        return pltpu.make_async_remote_copy(
            src_ref=self.row(source_rank),
            dst_ref=self.target.at[target_row],
            send_sem=self.send_sem.at[step],
            recv_sem=self.recv_sem.at[step],
            device_id=place_of(self.axis, device_rank),
            device_id_type=MESH,
        )

    def start(self):
        for step in range(1, self.size):
            rank = lax.rem(self.mine + step, self.size)
            self.copy(rank, self.mine, rank, step).start()

    def finish(self):
        for step in range(1, self.size):
            rank = lax.rem(self.mine + self.size - step, self.size)
            self.copy(self.mine, rank, rank, step).wait()


def place_of(axis, rank):
    if axis == "coil":
        return rank, lax.axis_index("slab")
    return lax.axis_index("coil"), rank


def greet():
    barrier = pltpu.get_barrier_semaphore()
    count = 0
    for axis in ("coil", "slab"):
        size = lax.axis_size(axis)
        for step in range(1, size):
            rank = lax.rem(lax.axis_index(axis) + step, size)
            pl.semaphore_signal(
                barrier, inc=1, device_id=place_of(axis, rank), device_id_type=MESH
            )
            count += 1
    return barrier, count


def high_low(table):
    high = np.asarray(table, np.float32).astype(jnp.bfloat16)
    return high, (np.asarray(table, np.float32) - high.astype(np.float32)).astype(jnp.bfloat16)


def fourier_tables(height, depth):
    def parts(length):
        counter = np.arange(length)
        angles = (counter[:, None] * counter[None, :] % length) * (2.0 * np.pi / length)
        return np.cos(angles) / np.sqrt(length), np.sin(angles) / np.sqrt(length)

    cos, sin = parts(depth)
    forward = np.block([[cos, -sin], [sin, cos]])
    backward = np.block([[cos, sin], [-sin, cos]])
    return high_low(forward) + high_low(backward) + high_low(np.concatenate(parts(height)))


def groups_of(slices, hidden):
    per = hidden // slices
    out = 4 if slices % 4 == 0 else slices
    spans = []
    for first in range(0, slices, out):
        low = max(first - 1, 0) * per // 32 * 32
        high = min(first + out + 1, slices) * per
        spans.append((low, high))
    width = -(-max(high - low for low, high in spans) // 128) * 128
    if width >= hidden:
        return slices, [0], hidden
    return out, [min(low, hidden - width) for low, _ in spans], width


def mid_eye(hidden, slices, start, width):
    lanes = start + np.arange(width)
    return np.arange(hidden // slices)[:, None] == lanes[None, :] % (hidden // slices)


def pack_constants(height, depth, slices, hidden, channels):
    outs, ins = hidden // slices, channels // slices
    _, starts, width = groups_of(slices, hidden)
    taps = 9
    rows = np.arange(taps * slices * ins)
    row_slice, row_part, row_tap = rows // ins % slices, rows % ins, rows // (slices * ins)
    lane_slice = np.arange(hidden) // outs
    items = {
        "eye": np.eye(outs),
        "spread": np.kron(np.eye(taps), np.tile(np.eye(ins), (1, slices))),
        "tile": np.tile(np.eye(outs), (1, slices)),
    }
    for index, start in enumerate(starts):
        items["mid", index] = mid_eye(hidden, slices, start, width)
    for flip in range(2):
        tap = taps - 1 - row_tap if flip else row_tap
        items["repeat", flip] = (
            np.arange(taps * ins)[None, :] == (tap * ins + row_part)[:, None]
        )
    for dx in range(3):
        items["band", dx] = lane_slice[None, :] == row_slice[:, None] + dx - 1
    names = ("ahead", "ahead_low", "back", "back_low", "down", "down_low")
    items.update(zip(names, fourier_tables(height, depth)))
    lanes = -(-max(item.shape[1] for item in items.values()) // 128) * 128
    places, blocks, at = {}, [], 0
    for name, item in items.items():
        count = -(-item.shape[0] // 16) * 16
        block = np.zeros((count, lanes), jnp.bfloat16)
        block[: item.shape[0], : item.shape[1]] = np.asarray(item).astype(jnp.bfloat16)
        places[name] = (at, item.shape)
        blocks.append(block)
        at += count
    return np.concatenate(blocks), places


def dot(left, right):
    return jnp.dot(left, right, preferred_element_type=f32)


def dot_nt(left, right):
    return lax.dot_general(left, right, (((1,), (1,)), ((), ())), preferred_element_type=f32)


def halves(values):
    high = values.astype(bf16)
    return high, (values - high.astype(f32)).astype(bf16)


def spectrum(values, get, inverse):
    height, depth = values.shape[0], values.shape[1] // 2
    names = ("back", "back_low") if inverse else ("ahead", "ahead_low")
    along_high, along_low = get(names[0]), get(names[1])
    down_high, down_low = get("down"), get("down_low")
    high, low = halves(values)
    high, low = halves(dot(high, along_high) + (dot(low, along_high) + dot(high, along_low)))
    both_parts = dot(down_high, high) + (dot(down_high, low) + dot(down_low, high))
    upper, lower = both_parts[:height], both_parts[height:]
    if inverse:
        return upper[:, :depth] - lower[:, depth:], lower[:, :depth] + upper[:, depth:]
    return upper[:, :depth] + lower[:, depth:], upper[:, depth:] - lower[:, :depth]


def coil_term(real, imag, coil, maps, kspace, mask, get):
    map_real, map_imag = maps[coil, 0, 0], maps[coil, 1, 0]
    image = jnp.concatenate(
        [map_real * real - map_imag * imag, map_real * imag + map_imag * real], axis=1
    )
    freq_real, freq_imag = spectrum(image, get, False)
    if kspace is not None:
        freq_real, freq_imag = freq_real - kspace[coil, 0, 0], freq_imag - kspace[coil, 1, 0]
    freq = jnp.concatenate([mask * freq_real, mask * freq_imag], axis=1)
    back_real, back_imag = spectrum(freq, get, True)
    return (
        map_real * back_real + map_imag * back_imag,
        map_real * back_imag - map_imag * back_real,
    )


def normal_part(real, imag, maps, kspace, mask, get):
    total = None
    for coil in range(maps.shape[0]):
        term = coil_term(real, imag, coil, maps, kspace, mask, get)
        total = term if total is None else (total[0] + term[0], total[1] + term[1])
    return total


def build_in(flat, flip, get, target, slices):
    outs = flat.shape[2]
    lane = lax.broadcasted_iota(jnp.int32, (outs, target.shape[1]), 1).astype(f32)
    ins = target.shape[1] // (9 * slices)
    lane_slice = jnp.floor((lane + 0.5) * (1.0 / ins))
    lane_slice = lane_slice - slices * jnp.floor((lane_slice + 0.5) * (1.0 / slices))
    wide = []
    for dx in range(3):
        turned = dot_nt(get("eye"), flat[2 - dx if flip else dx].astype(bf16)).astype(bf16)
        wide.append(dot(turned, get("spread")))
    for out_slice in range(slices):
        block = None
        for dx in range(3):
            term = jnp.where(lane_slice == float(out_slice + dx - 1), wide[dx], 0.0)
            block = term if block is None else block + term
        target[out_slice * outs : (out_slice + 1) * outs] = block.astype(bf16)


def build_out(flat, flip, get, target):
    total = None
    for dx in range(3):
        wide = dot(flat[2 - dx if flip else dx].astype(bf16), get("tile")).astype(bf16)
        term = dot(get(("repeat", flip)), wide) * get(("band", dx)).astype(f32)
        total = term if total is None else total + term
    target[...] = total.astype(bf16)


def build_mid(raw, flip, get, target, slices):
    outs, hidden = raw.shape[3], target.shape[0] * target.shape[1]
    out_count, starts, width = groups_of(slices, hidden)
    blocks = []
    for dx in range(3):
        for dy in range(3):
            for dz in range(3):
                if flip:
                    blocks.append(dot_nt(get("eye"), raw[2 - dx, 2 - dy, 2 - dz]))
                else:
                    blocks.append(raw[dx, dy, dz].astype(f32))
    stacked = jnp.concatenate(blocks, axis=0).astype(bf16)
    for index, start in enumerate(starts):
        wide = dot(stacked, get(("mid", index)))
        lane = lax.broadcasted_iota(jnp.int32, (outs, width), 1).astype(f32) + float(start)
        lane_slice = jnp.floor((lane + 0.5) * (1.0 / outs))
        for out_at in range(out_count):
            out_slice = index * out_count + out_at
            keeps = [lane_slice == float(out_slice + dx - 1) for dx in range(3)]
            for tap in range(9):
                block = None
                for dx in range(3):
                    at = (dx * 9 + tap) * outs
                    term = jnp.where(keeps[dx], wide[at : at + outs], 0.0)
                    block = term if block is None else block + term
                target[
                    index, out_at * outs : (out_at + 1) * outs, tap * width : (tap + 1) * width
                ] = block.astype(bf16)


def shifted(values, tap, depth):
    if tap == 1:
        return values
    lane = lax.broadcasted_iota(jnp.int32, (values.shape[0], depth), 1)
    edge, turn = (0, 1) if tap == 0 else (depth - 1, depth - 1)
    pieces = []
    for start in range(0, values.shape[1], depth):
        turned = pltpu.roll(values[:, start : start + depth], turn, 1)
        pieces.append(jnp.where(lane == edge, 0.0, turned))
    return jnp.concatenate(pieces, axis=1)


def conv_in(values, weights, depth):
    width = values.shape[1] - 2 * depth
    turned = [shifted(values, tap, depth) for tap in range(3)]
    stacked = jnp.concatenate(
        [turned[dz][:, dy * depth : dy * depth + width] for dy in range(3) for dz in range(3)],
        axis=0,
    )
    return dot(weights[...], stacked.astype(bf16))


def conv_mid(values, weights, depth, slices):
    cols = values.shape[1] - 2 * depth
    _, starts, width = groups_of(slices, values.shape[0])
    turned = [shifted(values, tap, depth).astype(bf16) for tap in range(3)]
    totals = []
    for index, start in enumerate(starts):
        stacked = jnp.concatenate(
            [
                turned[dz][start : start + width, dy * depth : dy * depth + cols]
                for dy in range(3)
                for dz in range(3)
            ],
            axis=0,
        )
        totals.append(dot(weights[index], stacked))
    return jnp.concatenate(totals, axis=0)


def conv_out(values, weights, depth):
    width = values.shape[1] - 2 * depth
    rows = weights.shape[0] // 9
    products = dot(weights[...], values.astype(bf16))
    total = None
    for dz in range(3):
        summed = None
        for dy in range(3):
            at = (dy * 3 + dz) * rows
            term = products[at : at + rows, dy * depth : dy * depth + width]
            summed = term if summed is None else summed + term
        term = shifted(summed, dz, depth)
        total = term if total is None else total + term
    return total


def step_kernel(places, *refs):
    (maps_in, kspace_in, mask_in, iterate_in, bits_in, loss_in, adjoint_in, first_in, second_in,
     last_in, table_in, new_out, probe_out, next_out, *refs) = refs
    (maps, kspace, mask, iterate, bits, loss, adjoint, raw_first, raw_second, raw_last, table,
     load_sem, *refs) = refs
    (outs, out_sem, padded, padded_iterate, padded_fields, padded_relaxed, flats, work, rows_work,
     own_iterate, own_fields, all_iterate, halo, parts_send, parts, window_send, windows,
     fields_send, fields, delta_send, delta, grads_send, grads_back, own_pulled, all_pulled,
     sums_send, sums, first, second, last, first_t, second_t, last_t, halo_sem, *sems) = refs
    channels = []
    for index, (axis, how, source, target) in enumerate((
        ("coil", "all", own_iterate, all_iterate),
        ("slab", "row", fields_send, fields),
        ("coil", "row", parts_send, parts),
        ("slab", "row", window_send, windows),
        ("slab", "row", delta_send, delta),
        ("slab", "row", grads_send.at[0], grads_back.at[0]),
        ("slab", "row", grads_send.at[1], grads_back.at[1]),
        ("coil", "all", own_pulled.at[0], all_pulled.at[0]),
        ("coil", "all", own_pulled.at[1], all_pulled.at[1]),
        ("coil", "row", sums_send.at[0], sums.at[0]),
        ("coil", "row", sums_send.at[1], sums.at[1]),
    )):
        channels.append(Channel(axis, how, source, target, sems[2 * index], sems[2 * index + 1]))
    (iterate_way, field_way, part_way, window_way, delta_way, *later) = channels
    grad_ways, pulled_ways, sum_ways = later[:2], later[2:4], later[4:]

    height, depth = mask.shape
    coils, _, rows, _ = all_iterate.shape
    slices, _, window, _ = windows.shape
    own = window - 2 * reach
    block = rows + 2 * reach
    my_coil, my_slab = lax.axis_index("coil"), lax.axis_index("slab")
    row_base = (my_coil * slices + my_slab) * own - reach
    coil_base = pl.multiple_of(my_coil * rows, 8)

    def get(name):
        at, shape = places[name]
        return table[at : at + shape[0], 0 : shape[1]]

    loads = {}
    tables_at = places["ahead"][0]
    for index, (name, source, target) in enumerate((
        ("iterate", iterate_in, iterate),
        ("bits", bits_in, bits),
        ("adjoint", adjoint_in, adjoint),
        ("second", second_in, raw_second),
        ("first", first_in, raw_first),
        ("last", last_in, raw_last),
        ("small", table_in.at[0:tables_at], table.at[0:tables_at]),
        ("maps", maps_in, maps),
        ("tables", table_in.at[tables_at:], table.at[tables_at:]),
        ("mask", mask_in, mask),
        ("kspace", kspace_in, kspace),
        ("loss", loss_in, loss),
    )):
        loads[name] = pltpu.make_async_copy(source, target, load_sem.at[index])
    barrier, arrivals = greet()
    for load in loads.values():
        load.start()
    edge = jnp.zeros((2, 8, depth), f32)
    for target in (padded, padded_iterate):
        target[:, 0:8] = edge
        target[:, height + reach : height + reach + 8] = edge
    loads["iterate"].wait()
    own_iterate[...] = iterate[:, 0].astype(bf16)
    pl.semaphore_wait(barrier, arrivals)
    iterate_way.start()
    loads["bits"].wait()
    loads["adjoint"].wait()
    own_fields[0:2] = (2 * bits[:, 0] - 1).astype(bf16)
    own_fields[2:4] = adjoint[:, 0].astype(bf16)
    halo_ways = []
    for side, (turn, at) in enumerate(((1, rows - 8), (coils - 1, 0))):
        halo_ways.append(
            pltpu.make_async_remote_copy(
                src_ref=own_fields.at[:, at : at + 8],
                dst_ref=halo.at[side],
                send_sem=halo_sem.at[side],
                recv_sem=halo_sem.at[2 + side],
                device_id=place_of("coil", lax.rem(my_coil + turn, coils)),
                device_id_type=MESH,
            )
        )
        halo_ways[-1].start()
    padded_fields[:, reach : reach + rows] = own_fields[...].astype(f32)
    for name in ("second", "first", "last", "small"):
        loads[name].wait()
    for side, raw in enumerate((raw_first, raw_last)):
        for dx in range(3):
            for tap in range(9):
                parts_of = raw[dx, tap // 3, tap % 3].astype(f32)
                flats[2 * side, dx, 2 * tap : 2 * tap + 2] = parts_of
                flats[2 * side + 1, dx, 16 - 2 * tap : 18 - 2 * tap] = parts_of
    build_in(flats.at[3], 1, get, last_t, slices)
    build_in(flats.at[0], 0, get, first, slices)
    build_mid(raw_second, 0, get, second, slices)
    build_mid(raw_second, 1, get, second_t, slices)
    build_out(flats.at[2], 0, get, last)
    build_out(flats.at[0], 1, get, first_t)
    for way in halo_ways:
        way.wait()
    keep = jnp.where(my_coil > 0, 1.0, 0.0).astype(f32)
    padded_fields[:, 0:reach] = halo[0, :, 8 - reach : 8].astype(f32) * keep
    keep = jnp.where(my_coil < coils - 1, 1.0, 0.0).astype(f32)
    padded_fields[:, reach + rows : block] = halo[1, :, 0:reach].astype(f32) * keep
    for piece in range(slices):
        fields_send[piece] = padded_fields[:, piece * own : piece * own + window].astype(bf16)
    field_way.start()
    for name in ("maps", "tables", "mask", "kspace"):
        loads[name].wait()
    weight = mask[...].astype(f32)
    all_iterate[my_coil] = own_iterate[...]
    iterate_way.finish()

    def column(gathered, channel):
        return jnp.concatenate(
            [gathered[piece, channel].astype(f32) for piece in range(coils)], axis=0
        )

    real, imag = column(all_iterate, 0), column(all_iterate, 1)
    total = normal_part(real, imag, maps, kspace, weight, get)
    padded[0, reach : reach + height] = total[0]
    padded[1, reach : reach + height] = total[1]
    for piece in range(coils):
        parts_send[piece] = padded[:, piece * rows : piece * rows + block].astype(bf16)
    part_way.start()
    padded_iterate[0, reach : reach + height] = real
    padded_iterate[1, reach : reach + height] = imag
    padded_relaxed[:, 0:block] = padded_iterate[:, pl.ds(coil_base, block)]
    padded_relaxed[:, reach : reach + rows] = iterate[:, 0]

    def load(values):
        work[...] = values.astype(f32).reshape(work.shape)
        return jnp.concatenate([work[:, row, :] for row in range(window)], axis=1)

    def cut(values, before, after):
        return values[:, before * depth : values.shape[1] - after * depth]

    def inside(values, offset):
        blocks = []
        for row in range(values.shape[1] // depth):
            at = row_base + offset + row
            keep = jnp.where((at >= 0) & (at < height), 1.0, 0.0).astype(f32)
            blocks.append(values[:, row * depth : (row + 1) * depth] * keep)
        return jnp.concatenate(blocks, axis=1)

    def store(values):
        for row in range(own):
            rows_work[:, row, :] = values[:, row * depth : (row + 1) * depth]
        return rows_work[...].reshape(slices, 2, own, depth).astype(bf16)

    fields[my_slab] = fields_send[my_slab]
    field_way.finish()
    grads = []
    for field in range(2):
        probe = cut(load(fields[:, 2 * field : 2 * field + 2]), 1, 1)
        grads.append(conv_in(probe, last_t, depth))
    part_way.finish()
    summed = padded[:, pl.ds(coil_base, block)]
    for step in range(1, coils):
        summed = summed + parts[lax.rem(my_coil + step, coils)].astype(f32)
    padded_relaxed[:, 0:block] = padded_relaxed[:, 0:block] - step_size * summed
    for piece in range(slices):
        window_send[piece] = padded_relaxed[:, piece * own : piece * own + window].astype(bf16)
    window_way.start()
    windows[my_slab] = window_send[my_slab]
    window_way.finish()

    pre1 = conv_in(load(windows[...]), first, depth)
    sig1 = jax.nn.sigmoid(pre1)
    act1 = inside(pre1 * sig1, 1)
    slope1 = inside(cut(sig1 * (1.0 + pre1 * (1.0 - sig1)), 2, 2), 3)
    pre2 = conv_mid(act1, second, depth, slices)
    sig2 = jax.nn.sigmoid(pre2)
    slope2 = inside(sig2 * (1.0 + pre2 * (1.0 - sig2)), 2)
    for field in range(2):
        grad1 = conv_mid(grads[field] * slope2, second_t, depth, slices) * slope1
        grads_send[field] = store(conv_out(grad1, first_t, depth))
        grad_ways[field].start()
        grads_back[field, my_slab] = grads_send[field, my_slab]
    act2 = inside(cut(pre2 * sig2, 1, 1), 3)
    delta_out = store(conv_out(act2, last, depth))

    exact = ((2 * bits[:, 0] - 1).astype(f32), adjoint[:, 0])
    pulled = []
    for field in range(2):
        grad_ways[field].finish()
        back = jnp.concatenate(
            [grads_back[field, piece].astype(f32) for piece in range(slices)], axis=1
        )
        pulled.append(exact[field] + back)
        own_pulled[field] = pulled[field].astype(bf16)
        pulled_ways[field].start()
        all_pulled[field, my_coil] = own_pulled[field]
        if field == 0:
            delta_send[...] = delta_out
            delta_way.start()
            delta[my_slab] = delta_send[my_slab]
    partial = []
    for field in range(2):
        pulled_ways[field].finish()
        real, imag = column(all_pulled.at[field], 0), column(all_pulled.at[field], 1)
        total = normal_part(real, imag, maps, None, weight, get)
        for part in range(2):
            padded[part, 0:height] = total[part]
            for piece in range(coils):
                sums_send[field, piece, part] = total[part][
                    piece * rows : (piece + 1) * rows
                ].astype(bf16)
        sum_ways[field].start()
        partial.append(padded[:, pl.ds(coil_base, rows)])

    results = (new_out, probe_out, next_out)
    finals = [
        pltpu.make_async_copy(outs.at[index], results[index], out_sem.at[index])
        for index in range(3)
    ]
    delta_way.finish()
    for piece in range(slices):
        at = piece * own
        outs[0, :, 0, at : at + own] = (
            padded_relaxed[:, reach + at : reach + at + own] + delta[piece].astype(f32)
        )
    finals[0].start()
    loads["loss"].wait()
    for field in range(2):
        sum_ways[field].finish()
        added = partial[field]
        for step in range(1, coils):
            added = added + sums[field, lax.rem(my_coil + step, coils)].astype(f32)
        value = pulled[field] - step_size * added
        outs[1 + field, :, 0] = value if field == 0 else loss[:, 0] + value
        finals[1 + field].start()
    for final in finals:
        final.wait()


def on_device(coil_maps, kspace, sample_mask, iterate, probe_bits, loss_gradient, adjoint,
              kernel_first, kernel_second, kernel_last):
    height, depth = sample_mask.shape
    coils, slabs = lax.axis_size("coil"), lax.axis_size("slab")
    own = height // (coils * slabs)
    window = own + 2 * reach
    rows = iterate.shape[2]
    block = rows + 2 * reach
    hidden, channels = kernel_second.shape[0] * slabs, kernel_first.shape[1] * slabs
    table, places = pack_constants(height, depth, slabs, hidden, channels)
    raws = (
        jnp.transpose(kernel_first, (2, 3, 4, 1, 0)),
        jnp.transpose(kernel_second, (2, 3, 4, 0, 1)),
        jnp.transpose(kernel_last, (2, 3, 4, 0, 1)),
    )
    operands = (coil_maps, kspace, sample_mask, iterate, probe_bits, loss_gradient, adjoint, *raws,
                jnp.asarray(table))
    _, starts, width = groups_of(slabs, hidden)
    mids = (len(starts), hidden // len(starts), 9 * width)
    image = jax.ShapeDtypeStruct(iterate.shape, f32)
    buffers = [
        ((2, height + 2 * reach + 8, depth), f32),
        ((2, height + 2 * reach + 8, depth), f32),
        ((4, block + 8, depth), f32),
        ((2, block + 8, depth), f32),
        ((4, 3, 18, kernel_second.shape[0]), f32),
        ((2 * slabs, window, depth), f32),
        ((2 * slabs, own, depth), f32),
        ((2, rows, depth), bf16),
        ((4, rows, depth), bf16),
        ((coils, 2, rows, depth), bf16),
        ((2, 4, 8, depth), bf16),
        ((coils, 2, block, depth), bf16),
        ((coils, 2, block, depth), bf16),
        ((slabs, 2, window, depth), bf16),
        ((slabs, 2, window, depth), bf16),
        ((slabs, 4, window, depth), bf16),
        ((slabs, 4, window, depth), bf16),
        ((slabs, 2, own, depth), bf16),
        ((slabs, 2, own, depth), bf16),
        ((2, slabs, 2, own, depth), bf16),
        ((2, slabs, 2, own, depth), bf16),
        ((2, 2, rows, depth), bf16),
        ((2, coils, 2, rows, depth), bf16),
        ((2, coils, 2, rows, depth), bf16),
        ((2, coils, 2, rows, depth), bf16),
        ((hidden, 9 * channels), bf16),
        (mids, bf16),
        ((9 * channels, hidden), bf16),
        ((9 * channels, hidden), bf16),
        (mids, bf16),
        ((hidden, 9 * channels), bf16),
    ]
    ways = (coils, slabs, coils, slabs, slabs, slabs, slabs, coils, coils, coils, coils)
    return pl.pallas_call(
        lambda *refs: step_kernel(places, *refs),
        out_shape=(image, image, image),
        in_specs=[in_hbm] * len(operands),
        out_specs=(anywhere,) * 3,
        scratch_shapes=[pltpu.VMEM(value.shape, value.dtype) for value in operands]
        + [pltpu.SemaphoreType.DMA((12,)), pltpu.VMEM((3, *iterate.shape), f32)]
        + [pltpu.SemaphoreType.DMA((3,))]
        + [pltpu.VMEM(shape, kind) for shape, kind in buffers]
        + [pltpu.SemaphoreType.DMA((4,))]
        + [pltpu.SemaphoreType.DMA((size,)) for size in ways for _ in range(2)],
        compiler_params=pltpu.CompilerParams(
            collective_id=0, has_side_effects=True, vmem_limit_bytes=66_800_000
        ),
        name="step",
    )(*operands)


def solution(mesh):
    split_coils = P("coil", None, "slab", None, None)
    image = P(None, "slab", "coil", None)
    return jax.shard_map(
        on_device,
        mesh=mesh,
        in_specs=(split_coils, split_coils, P(), image, image, image, image, P(), P(), P()),
        out_specs=(image, image, image),
        check_vma=False,
    )
```

```python
import jax
import jax.numpy as jnp
import numpy as np
from jax import lax
from jax.experimental import pallas as pl
from jax.experimental.pallas import tpu as pltpu
from jax.sharding import PartitionSpec as P

step_size = 0.8
reach = 4
f32 = jnp.float32
bf16 = jnp.bfloat16
in_hbm = pl.BlockSpec(memory_space=pltpu.HBM)
in_vmem = pl.BlockSpec(memory_space=pltpu.VMEM)
MESH = pl.DeviceIdType.MESH


class Channel:
    def __init__(self, axis, how, source, target, send_sem, recv_sem):
        self.axis, self.how, self.source, self.target = axis, how, source, target
        self.send_sem, self.recv_sem = send_sem, recv_sem
        self.size, self.mine = lax.axis_size(axis), lax.axis_index(axis)

    def row(self, rank):
        return self.source if self.how == "all" else self.source.at[rank]

    def copy(self, source_rank, target_row, device_rank, step):
        return pltpu.make_async_remote_copy(
            src_ref=self.row(source_rank),
            dst_ref=self.target.at[target_row],
            send_sem=self.send_sem.at[step],
            recv_sem=self.recv_sem.at[step],
            device_id=place_of(self.axis, device_rank),
            device_id_type=MESH,
        )

    def start(self):
        for step in range(1, self.size):
            rank = lax.rem(self.mine + step, self.size)
            self.copy(rank, self.mine, rank, step).start()

    def finish(self):
        for step in range(1, self.size):
            rank = lax.rem(self.mine + self.size - step, self.size)
            self.copy(self.mine, rank, rank, step).wait()


def place_of(axis, rank):
    if axis == "coil":
        return rank, lax.axis_index("slab")
    return lax.axis_index("coil"), rank


def greet():
    barrier = pltpu.get_barrier_semaphore()
    count = 0
    for axis in ("coil", "slab"):
        size = lax.axis_size(axis)
        for step in range(1, size):
            rank = lax.rem(lax.axis_index(axis) + step, size)
            pl.semaphore_signal(
                barrier, inc=1, device_id=place_of(axis, rank), device_id_type=MESH
            )
            count += 1
    return barrier, count


def high_low(table):
    high = np.asarray(table, np.float32).astype(jnp.bfloat16)
    return high, (np.asarray(table, np.float32) - high.astype(np.float32)).astype(jnp.bfloat16)


def fourier_tables(height, depth):
    def parts(length):
        counter = np.arange(length)
        angles = (counter[:, None] * counter[None, :] % length) * (2.0 * np.pi / length)
        return np.cos(angles) / np.sqrt(length), np.sin(angles) / np.sqrt(length)

    cos, sin = parts(depth)
    forward = np.block([[cos, -sin], [sin, cos]])
    backward = np.block([[cos, sin], [-sin, cos]])
    return high_low(forward) + high_low(backward) + high_low(np.concatenate(parts(height)))


def groups_of(slices, hidden):
    per = hidden // slices
    out = 4 if slices % 4 == 0 else slices
    spans = []
    for first in range(0, slices, out):
        low = max(first - 1, 0) * per // 32 * 32
        high = min(first + out + 1, slices) * per
        spans.append((low, high))
    width = -(-max(high - low for low, high in spans) // 128) * 128
    if width >= hidden:
        return slices, [0], hidden
    return out, [min(low, hidden - width) for low, _ in spans], width


def mid_eye(hidden, slices, start, width):
    lanes = start + np.arange(width)
    return np.arange(hidden // slices)[:, None] == lanes[None, :] % (hidden // slices)


def pack_constants(height, depth, slices, hidden, channels):
    outs, ins = hidden // slices, channels // slices
    _, starts, width = groups_of(slices, hidden)
    taps = 9
    rows = np.arange(taps * slices * ins)
    row_slice, row_part, row_tap = rows // ins % slices, rows % ins, rows // (slices * ins)
    lane_slice = np.arange(hidden) // outs
    items = {
        "eye": np.eye(outs),
        "spread": np.kron(np.eye(taps), np.tile(np.eye(ins), (1, slices))),
        "tile": np.tile(np.eye(outs), (1, slices)),
    }
    for index, start in enumerate(starts):
        items["mid", index] = mid_eye(hidden, slices, start, width)
    for flip in range(2):
        tap = taps - 1 - row_tap if flip else row_tap
        items["repeat", flip] = (
            np.arange(taps * ins)[None, :] == (tap * ins + row_part)[:, None]
        )
    for dx in range(3):
        items["band", dx] = lane_slice[None, :] == row_slice[:, None] + dx - 1
    names = ("ahead", "ahead_low", "back", "back_low", "down", "down_low")
    items.update(zip(names, fourier_tables(height, depth)))
    lanes = -(-max(item.shape[1] for item in items.values()) // 128) * 128
    places, blocks, at = {}, [], 0
    for name, item in items.items():
        count = -(-item.shape[0] // 16) * 16
        block = np.zeros((count, lanes), jnp.bfloat16)
        block[: item.shape[0], : item.shape[1]] = np.asarray(item).astype(jnp.bfloat16)
        places[name] = (at, item.shape)
        blocks.append(block)
        at += count
    return np.concatenate(blocks), places


def dot(left, right):
    return jnp.dot(left, right, preferred_element_type=f32)


def dot_nt(left, right):
    return lax.dot_general(left, right, (((1,), (1,)), ((), ())), preferred_element_type=f32)


def halves(values):
    high = values.astype(bf16)
    return high, (values - high.astype(f32)).astype(bf16)


def spectrum(values, get, inverse, fine):
    height, depth = values.shape[0], values.shape[1] // 2
    names = ("back", "back_low") if inverse else ("ahead", "ahead_low")
    high, low = halves(values)
    turned = dot(high, get(names[0]))
    if fine:
        turned = turned + (dot(low, get(names[0])) + dot(high, get(names[1])))
    high, low = halves(turned)
    both_parts = dot(get("down"), high)
    if fine:
        both_parts = both_parts + (dot(get("down"), low) + dot(get("down_low"), high))
    upper, lower = both_parts[:height], both_parts[height:]
    if inverse:
        return upper[:, :depth] - lower[:, depth:], lower[:, :depth] + upper[:, depth:]
    return upper[:, :depth] + lower[:, depth:], upper[:, depth:] - lower[:, :depth]


def coil_term(real, imag, coil, maps, kspace, mask, get):
    map_real, map_imag = maps[coil, 0, 0], maps[coil, 1, 0]
    image = jnp.concatenate(
        [map_real * real - map_imag * imag, map_real * imag + map_imag * real], axis=1
    )
    freq_real, freq_imag = spectrum(image, get, False, False)
    if kspace is not None:
        freq_real, freq_imag = freq_real - kspace[coil, 0, 0], freq_imag - kspace[coil, 1, 0]
    freq = jnp.concatenate([mask * freq_real, mask * freq_imag], axis=1)
    back_real, back_imag = spectrum(freq, get, True, kspace is not None)
    return (
        map_real * back_real + map_imag * back_imag,
        map_real * back_imag - map_imag * back_real,
    )


def normal_part(real, imag, maps, kspace, mask, get):
    total = None
    for coil in range(maps.shape[0]):
        term = coil_term(real, imag, coil, maps, kspace, mask, get)
        total = term if total is None else (total[0] + term[0], total[1] + term[1])
    return total


def build_in(flat, flip, get, target, slices):
    outs = flat.shape[2]
    lane = lax.broadcasted_iota(jnp.int32, (outs, target.shape[1]), 1).astype(f32)
    ins = target.shape[1] // (9 * slices)
    lane_slice = jnp.floor((lane + 0.5) * (1.0 / ins))
    lane_slice = lane_slice - slices * jnp.floor((lane_slice + 0.5) * (1.0 / slices))
    wide = []
    for dx in range(3):
        turned = dot_nt(get("eye"), flat[2 - dx if flip else dx].astype(bf16)).astype(bf16)
        wide.append(dot(turned, get("spread")))
    for out_slice in range(slices):
        block = None
        for dx in range(3):
            term = jnp.where(lane_slice == float(out_slice + dx - 1), wide[dx], 0.0)
            block = term if block is None else block + term
        target[out_slice * outs : (out_slice + 1) * outs] = block.astype(bf16)


def build_out(flat, flip, get, target):
    total = None
    for dx in range(3):
        wide = dot(flat[2 - dx if flip else dx].astype(bf16), get("tile")).astype(bf16)
        term = dot(get(("repeat", flip)), wide) * get(("band", dx)).astype(f32)
        total = term if total is None else total + term
    target[...] = total.astype(bf16)


def build_mid(raw, flip, get, target, slices):
    outs, hidden = raw.shape[3], target.shape[0] * target.shape[1]
    out_count, starts, width = groups_of(slices, hidden)
    blocks = []
    for dx in range(3):
        for dy in range(3):
            for dz in range(3):
                if flip:
                    blocks.append(dot_nt(get("eye"), raw[2 - dx, 2 - dy, 2 - dz]))
                else:
                    blocks.append(raw[dx, dy, dz].astype(f32))
    stacked = jnp.concatenate(blocks, axis=0).astype(bf16)
    for index, start in enumerate(starts):
        wide = dot(stacked, get(("mid", index)))
        lane = lax.broadcasted_iota(jnp.int32, (outs, width), 1).astype(f32) + float(start)
        lane_slice = jnp.floor((lane + 0.5) * (1.0 / outs))
        for out_at in range(out_count):
            out_slice = index * out_count + out_at
            keeps = [lane_slice == float(out_slice + dx - 1) for dx in range(3)]
            for tap in range(9):
                block = None
                for dx in range(3):
                    at = (dx * 9 + tap) * outs
                    term = jnp.where(keeps[dx], wide[at : at + outs], 0.0)
                    block = term if block is None else block + term
                target[
                    index, out_at * outs : (out_at + 1) * outs, tap * width : (tap + 1) * width
                ] = block.astype(bf16)


def shifted(values, tap, depth):
    if tap == 1:
        return values
    lane = lax.broadcasted_iota(jnp.int32, (values.shape[0], depth), 1)
    edge, turn = (0, 1) if tap == 0 else (depth - 1, depth - 1)
    pieces = []
    for start in range(0, values.shape[1], depth):
        turned = pltpu.roll(values[:, start : start + depth], turn, 1)
        pieces.append(jnp.where(lane == edge, 0.0, turned))
    return jnp.concatenate(pieces, axis=1)


def conv_in(values, weights, depth):
    width = values.shape[1] - 2 * depth
    turned = [shifted(values, tap, depth) for tap in range(3)]
    stacked = jnp.concatenate(
        [turned[dz][:, dy * depth : dy * depth + width] for dy in range(3) for dz in range(3)],
        axis=0,
    )
    return dot(weights[...], stacked.astype(bf16))


def conv_mid(values, weights, depth, slices):
    cols = values.shape[1] - 2 * depth
    _, starts, width = groups_of(slices, values.shape[0])
    turned = [shifted(values, tap, depth).astype(bf16) for tap in range(3)]
    totals = []
    for index, start in enumerate(starts):
        stacked = jnp.concatenate(
            [
                turned[dz][start : start + width, dy * depth : dy * depth + cols]
                for dy in range(3)
                for dz in range(3)
            ],
            axis=0,
        )
        totals.append(dot(weights[index], stacked))
    return jnp.concatenate(totals, axis=0)


def conv_out(values, weights, depth):
    width = values.shape[1] - 2 * depth
    rows = weights.shape[0] // 9
    products = dot(weights[...], values.astype(bf16))
    total = None
    for dz in range(3):
        summed = None
        for dy in range(3):
            at = (dy * 3 + dz) * rows
            term = products[at : at + rows, dy * depth : dy * depth + width]
            summed = term if summed is None else summed + term
        term = shifted(summed, dz, depth)
        total = term if total is None else total + term
    return total


def sigmoid(values):
    return 0.5 + 0.5 * jnp.tanh(0.5 * values)


def step_kernel(places, *refs):
    (maps_in, kspace_in, mask_in, iterate_in, bits_in, adjoint_in, first_in, second_in,
     last_in, table_in, result, *refs) = refs
    (maps, kspace, mask, iterate, bits, adjoint, raw_first, raw_second, raw_last, table,
     load_sem, *refs) = refs
    (padded, padded_iterate, padded_fields, padded_relaxed, flats, work, rows_work,
     own_iterate, own_fields, all_iterate, halo, parts_send, parts, window_send, windows,
     fields_send, fields, delta_send, delta, grads_send, grads_back, own_pulled, all_pulled,
     sums_send, sums, first, second, last, first_t, second_t, last_t, halo_sem, *sems) = refs
    channels = []
    for index, (axis, how, source, target) in enumerate((
        ("coil", "all", own_iterate, all_iterate),
        ("slab", "row", fields_send, fields),
        ("coil", "row", parts_send, parts),
        ("slab", "row", window_send, windows),
        ("slab", "row", delta_send, delta),
        ("slab", "row", grads_send.at[0], grads_back.at[0]),
        ("slab", "row", grads_send.at[1], grads_back.at[1]),
        ("coil", "all", own_pulled.at[0], all_pulled.at[0]),
        ("coil", "all", own_pulled.at[1], all_pulled.at[1]),
        ("coil", "row", sums_send.at[0], sums.at[0]),
        ("coil", "row", sums_send.at[1], sums.at[1]),
    )):
        channels.append(Channel(axis, how, source, target, sems[2 * index], sems[2 * index + 1]))
    (iterate_way, field_way, part_way, window_way, delta_way, *later) = channels
    grad_ways, pulled_ways, sum_ways = later[:2], later[2:4], later[4:]

    height, depth = mask.shape
    coils, _, rows, _ = all_iterate.shape
    slices, _, window, _ = windows.shape
    own = window - 2 * reach
    block = rows + 2 * reach
    my_coil, my_slab = lax.axis_index("coil"), lax.axis_index("slab")
    row_base = (my_coil * slices + my_slab) * own - reach
    coil_base = pl.multiple_of(my_coil * rows, 8)

    def get(name):
        at, shape = places[name]
        return table[at : at + shape[0], 0 : shape[1]]

    loads = {}
    tables_at = places["ahead"][0]
    for index, (name, source, target) in enumerate((
        ("iterate", iterate_in, iterate),
        ("bits", bits_in, bits),
        ("adjoint", adjoint_in, adjoint),
        ("second", second_in, raw_second),
        ("first", first_in, raw_first),
        ("last", last_in, raw_last),
        ("small", table_in.at[0:tables_at], table.at[0:tables_at]),
        ("maps", maps_in, maps),
        ("tables", table_in.at[tables_at:], table.at[tables_at:]),
        ("mask", mask_in, mask),
        ("kspace", kspace_in, kspace),
    )):
        loads[name] = pltpu.make_async_copy(source, target, load_sem.at[index])
    barrier, arrivals = greet()
    for load in loads.values():
        load.start()
    edge = jnp.zeros((2, 8, depth), f32)
    for target in (padded, padded_iterate):
        target[:, 0:8] = edge
        target[:, height + reach : height + reach + 8] = edge
    loads["iterate"].wait()
    own_iterate[...] = iterate[:, 0].astype(bf16)
    pl.semaphore_wait(barrier, arrivals)
    iterate_way.start()
    loads["bits"].wait()
    loads["adjoint"].wait()
    own_fields[0:2] = (2 * bits[:, 0] - 1).astype(bf16)
    own_fields[2:4] = adjoint[:, 0].astype(bf16)
    halo_ways = []
    for side, (turn, at) in enumerate(((1, rows - 8), (coils - 1, 0))):
        halo_ways.append(
            pltpu.make_async_remote_copy(
                src_ref=own_fields.at[:, at : at + 8],
                dst_ref=halo.at[side],
                send_sem=halo_sem.at[side],
                recv_sem=halo_sem.at[2 + side],
                device_id=place_of("coil", lax.rem(my_coil + turn, coils)),
                device_id_type=MESH,
            )
        )
        halo_ways[-1].start()
    for name in ("second", "first", "last", "small"):
        loads[name].wait()
    for side, raw in enumerate((raw_first, raw_last)):
        for dx in range(3):
            for tap in range(9):
                parts_of = raw[dx, tap // 3, tap % 3].astype(f32)
                flats[2 * side, dx, 2 * tap : 2 * tap + 2] = parts_of
                flats[2 * side + 1, dx, 16 - 2 * tap : 18 - 2 * tap] = parts_of
    build_in(flats.at[3], 1, get, last_t, slices)
    build_in(flats.at[0], 0, get, first, slices)
    build_mid(raw_second, 0, get, second, slices)
    build_mid(raw_second, 1, get, second_t, slices)
    for name in ("maps", "tables", "mask", "kspace"):
        loads[name].wait()
    weight = mask[...].astype(f32)
    all_iterate[my_coil] = own_iterate[...]
    iterate_way.finish()

    def column(gathered, channel):
        return jnp.concatenate(
            [gathered[piece, channel].astype(f32) for piece in range(coils)], axis=0
        )

    real, imag = column(all_iterate, 0), column(all_iterate, 1)
    total = normal_part(real, imag, maps, kspace, weight, get)
    padded[0, reach : reach + height] = total[0]
    padded[1, reach : reach + height] = total[1]
    for piece in range(coils):
        parts_send[piece] = padded[:, piece * rows : piece * rows + block].astype(bf16)
    part_way.start()
    padded_fields[:, reach : reach + rows] = own_fields[...].astype(f32)
    for way in halo_ways:
        way.wait()
    keep = jnp.where(my_coil > 0, 1.0, 0.0).astype(f32)
    padded_fields[:, 0:reach] = halo[0, :, 8 - reach : 8].astype(f32) * keep
    keep = jnp.where(my_coil < coils - 1, 1.0, 0.0).astype(f32)
    padded_fields[:, reach + rows : block] = halo[1, :, 0:reach].astype(f32) * keep
    for piece in range(slices):
        fields_send[piece] = padded_fields[:, piece * own : piece * own + window].astype(bf16)
    field_way.start()
    padded_iterate[0, reach : reach + height] = real
    padded_iterate[1, reach : reach + height] = imag
    padded_relaxed[:, 0:block] = padded_iterate[:, pl.ds(coil_base, block)]
    padded_relaxed[:, reach : reach + rows] = iterate[:, 0]

    def load(values):
        work[...] = values.astype(f32).reshape(work.shape)
        return jnp.concatenate([work[:, row, :] for row in range(window)], axis=1)

    def cut(values, before, after):
        return values[:, before * depth : values.shape[1] - after * depth]

    def inside(values, offset):
        blocks = []
        for row in range(values.shape[1] // depth):
            at = row_base + offset + row
            keep = jnp.where((at >= 0) & (at < height), 1.0, 0.0).astype(f32)
            blocks.append(values[:, row * depth : (row + 1) * depth] * keep)
        return jnp.concatenate(blocks, axis=1)

    def store(values):
        for row in range(own):
            rows_work[:, row, :] = values[:, row * depth : (row + 1) * depth]
        return rows_work[...].reshape(slices, 2, own, depth).astype(bf16)

    build_out(flats.at[2], 0, get, last)
    build_out(flats.at[0], 1, get, first_t)
    part_way.finish()
    summed = padded[:, pl.ds(coil_base, block)]
    for step in range(1, coils):
        summed = summed + parts[lax.rem(my_coil + step, coils)].astype(f32)
    padded_relaxed[:, 0:block] = padded_relaxed[:, 0:block] - step_size * summed
    for piece in range(slices):
        window_send[piece] = padded_relaxed[:, piece * own : piece * own + window].astype(bf16)
    window_way.start()
    windows[my_slab] = window_send[my_slab]
    fields[my_slab] = fields_send[my_slab]
    field_way.finish()
    grads = []
    for field in range(2):
        probe = cut(load(fields[:, 2 * field : 2 * field + 2]), 1, 1)
        grads.append(conv_in(probe, last_t, depth))
    window_way.finish()

    pre1 = conv_in(load(windows[...]), first, depth)
    sig1 = sigmoid(pre1)
    act1 = pre1 * sig1
    slope1 = inside(cut(sig1 + act1 * (1.0 - sig1), 2, 2), 3)
    act1 = inside(act1, 1)
    pre2 = conv_mid(act1, second, depth, slices)
    sig2 = sigmoid(pre2)
    act2 = pre2 * sig2
    slope2 = inside(sig2 + act2 * (1.0 - sig2), 2)
    for field in range(2):
        grad1 = conv_mid(grads[field] * slope2, second_t, depth, slices) * slope1
        grads_send[field] = store(conv_out(grad1, first_t, depth))
        grad_ways[field].start()
        grads_back[field, my_slab] = grads_send[field, my_slab]
    act2 = inside(cut(act2, 1, 1), 3)
    delta_out = store(conv_out(act2, last, depth))

    exact = ((2 * bits[:, 0] - 1).astype(f32), adjoint[:, 0])
    backs = []
    for field in range(2):
        grad_ways[field].finish()
        back = jnp.concatenate(
            [grads_back[field, piece].astype(f32) for piece in range(slices)], axis=1
        )
        backs.append(back)
        own_pulled[field] = (exact[field] + back).astype(bf16)
        pulled_ways[field].start()
        all_pulled[field, my_coil] = own_pulled[field]
        if field == 0:
            delta_send[...] = delta_out
            delta_way.start()
            delta[my_slab] = delta_send[my_slab]
    partial = []
    for field in range(2):
        pulled_ways[field].finish()
        real, imag = column(all_pulled.at[field], 0), column(all_pulled.at[field], 1)
        total = normal_part(real, imag, maps, None, weight, get)
        for part in range(2):
            padded[part, 0:height] = total[part]
            for piece in range(coils):
                sums_send[field, piece, part] = total[part][
                    piece * rows : (piece + 1) * rows
                ].astype(bf16)
        sum_ways[field].start()
        partial.append(padded[:, pl.ds(coil_base, rows)])

    delta_way.finish()
    for piece in range(slices):
        at = piece * own
        result[0, :, at : at + own] = (
            padded_relaxed[:, reach + at : reach + at + own] - iterate[:, 0, at : at + own]
        ) + delta[piece].astype(f32)
    for field in range(2):
        sum_ways[field].finish()
        added = partial[field]
        for step in range(1, coils):
            added = added + sums[field, lax.rem(my_coil + step, coils)].astype(f32)
        result[1 + field] = backs[field] - step_size * added


def on_device(coil_maps, kspace, sample_mask, iterate, probe_bits, loss_gradient, adjoint,
              kernel_first, kernel_second, kernel_last):
    height, depth = sample_mask.shape
    coils, slabs = lax.axis_size("coil"), lax.axis_size("slab")
    own = height // (coils * slabs)
    window = own + 2 * reach
    rows = iterate.shape[2]
    block = rows + 2 * reach
    hidden, channels = kernel_second.shape[0] * slabs, kernel_first.shape[1] * slabs
    table, places = pack_constants(height, depth, slabs, hidden, channels)
    raws = (
        jnp.transpose(kernel_first, (2, 3, 4, 1, 0)),
        jnp.transpose(kernel_second, (2, 3, 4, 0, 1)),
        jnp.transpose(kernel_last, (2, 3, 4, 0, 1)),
    )
    operands = (coil_maps, kspace, sample_mask, iterate, probe_bits, adjoint, *raws,
                jnp.asarray(table))
    _, starts, width = groups_of(slabs, hidden)
    mids = (len(starts), hidden // len(starts), 9 * width)
    buffers = [
        ((2, height + 2 * reach + 8, depth), f32),
        ((2, height + 2 * reach + 8, depth), f32),
        ((4, block + 8, depth), f32),
        ((2, block + 8, depth), f32),
        ((4, 3, 18, kernel_second.shape[0]), f32),
        ((2 * slabs, window, depth), f32),
        ((2 * slabs, own, depth), f32),
        ((2, rows, depth), bf16),
        ((4, rows, depth), bf16),
        ((coils, 2, rows, depth), bf16),
        ((2, 4, 8, depth), bf16),
        ((coils, 2, block, depth), bf16),
        ((coils, 2, block, depth), bf16),
        ((slabs, 2, window, depth), bf16),
        ((slabs, 2, window, depth), bf16),
        ((slabs, 4, window, depth), bf16),
        ((slabs, 4, window, depth), bf16),
        ((slabs, 2, own, depth), bf16),
        ((slabs, 2, own, depth), bf16),
        ((2, slabs, 2, own, depth), bf16),
        ((2, slabs, 2, own, depth), bf16),
        ((2, 2, rows, depth), bf16),
        ((2, coils, 2, rows, depth), bf16),
        ((2, coils, 2, rows, depth), bf16),
        ((2, coils, 2, rows, depth), bf16),
        ((hidden, 9 * channels), bf16),
        (mids, bf16),
        ((9 * channels, hidden), bf16),
        ((9 * channels, hidden), bf16),
        (mids, bf16),
        ((hidden, 9 * channels), bf16),
    ]
    ways = (coils, slabs, coils, slabs, slabs, slabs, slabs, coils, coils, coils, coils)
    changes = pl.pallas_call(
        lambda *refs: step_kernel(places, *refs),
        out_shape=pltpu.VMEM((3, 2, rows, depth), f32),
        in_specs=[in_hbm] * len(operands),
        out_specs=in_vmem,
        scratch_shapes=[pltpu.VMEM(value.shape, value.dtype) for value in operands]
        + [pltpu.SemaphoreType.DMA((11,))]
        + [pltpu.VMEM(shape, kind) for shape, kind in buffers]
        + [pltpu.SemaphoreType.DMA((4,))]
        + [pltpu.SemaphoreType.DMA((size,)) for size in ways for _ in range(2)],
        compiler_params=pltpu.CompilerParams(
            collective_id=0, has_side_effects=True, vmem_limit_bytes=40 << 20
        ),
        name="step",
    )(*[pltpu.with_memory_space_constraint(value, pltpu.HBM) for value in operands])
    changes = changes[:, :, None]
    sign = (2 * probe_bits - 1).astype(f32)
    return iterate + changes[0], sign + changes[1], loss_gradient + (adjoint + changes[2])


def solution(mesh):
    split_coils = P("coil", None, "slab", None, None)
    image = P(None, "slab", "coil", None)
    return jax.shard_map(
        on_device,
        mesh=mesh,
        in_specs=(split_coils, split_coils, P(), image, image, image, image, P(), P(), P()),
        out_specs=(image, image, image),
        check_vma=False,
    )
```

```python
import jax
import jax.numpy as jnp
import numpy as np
from jax import lax
from jax.experimental import pallas as pl
from jax.experimental.pallas import tpu as pltpu
from jax.sharding import PartitionSpec as P

step_size = 0.8
reach = 4
f32 = jnp.float32
bf16 = jnp.bfloat16
in_hbm = pl.BlockSpec(memory_space=pltpu.HBM)
in_vmem = pl.BlockSpec(memory_space=pltpu.VMEM)
MESH = pl.DeviceIdType.MESH


class Channel:
    def __init__(self, axis, how, source, target, send_sem, recv_sem):
        self.axis, self.how, self.source, self.target = axis, how, source, target
        self.send_sem, self.recv_sem = send_sem, recv_sem
        self.size, self.mine = lax.axis_size(axis), lax.axis_index(axis)

    def row(self, rank):
        return self.source if self.how == "all" else self.source.at[rank]

    def copy(self, source_rank, target_row, device_rank):
        return pltpu.make_async_remote_copy(
            src_ref=self.row(source_rank),
            dst_ref=self.target.at[target_row],
            send_sem=self.send_sem,
            recv_sem=self.recv_sem,
            device_id=place_of(self.axis, device_rank),
            device_id_type=MESH,
        )

    def start(self):
        for step in range(1, self.size):
            rank = lax.rem(self.mine + step, self.size)
            self.copy(rank, self.mine, rank).start()

    def finish(self):
        landed = self.target.at[0 : self.size - 1]
        for sem in (self.send_sem, self.recv_sem):
            pltpu.make_async_copy(landed, landed, sem).wait()


def place_of(axis, rank):
    if axis == "coil":
        return rank, lax.axis_index("slab")
    return lax.axis_index("coil"), rank


def greet():
    barrier = pltpu.get_barrier_semaphore()
    count = 0
    for axis in ("coil", "slab"):
        size = lax.axis_size(axis)
        for step in range(1, size):
            rank = lax.rem(lax.axis_index(axis) + step, size)
            pl.semaphore_signal(
                barrier, inc=1, device_id=place_of(axis, rank), device_id_type=MESH
            )
            count += 1
    return barrier, count


def high_low(table):
    high = np.asarray(table, np.float32).astype(jnp.bfloat16)
    return high, (np.asarray(table, np.float32) - high.astype(np.float32)).astype(jnp.bfloat16)


def fourier_tables(height, depth):
    def parts(length):
        counter = np.arange(length)
        angles = (counter[:, None] * counter[None, :] % length) * (2.0 * np.pi / length)
        return np.cos(angles) / np.sqrt(length), np.sin(angles) / np.sqrt(length)

    cos, sin = parts(depth)
    forward = np.block([[cos, -sin], [sin, cos]])
    backward = np.block([[cos, sin], [-sin, cos]])
    return high_low(forward) + high_low(backward) + high_low(np.concatenate(parts(height)))


def groups_of(slices, hidden):
    per = hidden // slices
    out = 4 if slices % 4 == 0 else slices
    spans = []
    for first in range(0, slices, out):
        low = max(first - 1, 0) * per // 32 * 32
        high = min(first + out + 1, slices) * per
        spans.append((low, high))
    width = -(-max(high - low for low, high in spans) // 128) * 128
    if width >= hidden:
        return slices, [0], hidden
    return out, [min(low, hidden - width) for low, _ in spans], width


def mid_eye(hidden, slices, start, width):
    lanes = start + np.arange(width)
    return np.arange(hidden // slices)[:, None] == lanes[None, :] % (hidden // slices)


def pack_constants(height, depth, slices, hidden, channels):
    outs, ins = hidden // slices, channels // slices
    _, starts, width = groups_of(slices, hidden)
    taps = 9
    rows = np.arange(taps * slices * ins)
    row_slice, row_part, row_tap = rows // ins % slices, rows % ins, rows // (slices * ins)
    lane_slice = np.arange(hidden) // outs
    items = {
        "eye": np.eye(outs),
        "spread": np.kron(np.eye(taps), np.tile(np.eye(ins), (1, slices))),
        "tile": np.tile(np.eye(outs), (1, slices)),
    }
    for index, start in enumerate(starts):
        items["mid", index] = mid_eye(hidden, slices, start, width)
    for flip in range(2):
        tap = taps - 1 - row_tap if flip else row_tap
        items["repeat", flip] = (
            np.arange(taps * ins)[None, :] == (tap * ins + row_part)[:, None]
        )
    for dx in range(3):
        items["band", dx] = lane_slice[None, :] == row_slice[:, None] + dx - 1
    names = ("ahead", "ahead_low", "back", "back_low", "down", "down_low")
    items.update(zip(names, fourier_tables(height, depth)))
    lanes = -(-max(item.shape[1] for item in items.values()) // 128) * 128
    places, blocks, at = {}, [], 0
    for name, item in items.items():
        count = -(-item.shape[0] // 16) * 16
        block = np.zeros((count, lanes), jnp.bfloat16)
        block[: item.shape[0], : item.shape[1]] = np.asarray(item).astype(jnp.bfloat16)
        places[name] = (at, item.shape)
        blocks.append(block)
        at += count
    return np.concatenate(blocks), places


def dot(left, right):
    return jnp.dot(left, right, preferred_element_type=f32)


def dot_nt(left, right):
    return lax.dot_general(left, right, (((1,), (1,)), ((), ())), preferred_element_type=f32)


def halves(values):
    high = values.astype(bf16)
    return high, (values - high.astype(f32)).astype(bf16)


def spectrum(images, get, inverse, fine):
    count, height, depth = len(images), images[0].shape[0], images[0].shape[1] // 2
    names = ("back", "back_low") if inverse else ("ahead", "ahead_low")
    high, low = halves(jnp.concatenate(images, axis=0))
    turned = dot(high, get(names[0]))
    if fine:
        turned = turned + (dot(low, get(names[0])) + dot(high, get(names[1])))
    turned = jnp.concatenate(
        [turned[at * height : (at + 1) * height] for at in range(count)], axis=1
    )
    high = turned.astype(bf16)
    both_parts = dot(get("down"), high)
    results = []
    for at in range(count):
        start = 2 * at * depth
        upper = both_parts[:height, start : start + 2 * depth]
        lower = both_parts[height:, start : start + 2 * depth]
        if inverse:
            results.append(
                (upper[:, :depth] - lower[:, depth:], lower[:, :depth] + upper[:, depth:])
            )
        else:
            results.append(
                (upper[:, :depth] + lower[:, depth:], upper[:, depth:] - lower[:, :depth])
            )
    return results


def normal_part(real, imag, maps, kspace, mask, get):
    images = []
    for coil in range(maps.shape[0]):
        map_real, map_imag = maps[coil, 0, 0], maps[coil, 1, 0]
        images.append(
            jnp.concatenate(
                [map_real * real - map_imag * imag, map_real * imag + map_imag * real], axis=1
            )
        )
    masked = []
    for coil, (freq_real, freq_imag) in enumerate(spectrum(images, get, False, False)):
        if kspace is not None:
            freq_real = freq_real - kspace[coil, 0, 0]
            freq_imag = freq_imag - kspace[coil, 1, 0]
        masked.append(jnp.concatenate([mask * freq_real, mask * freq_imag], axis=1))
    total = None
    for coil, (real, imag) in enumerate(spectrum(masked, get, True, kspace is not None)):
        map_real, map_imag = maps[coil, 0, 0], maps[coil, 1, 0]
        term = (map_real * real + map_imag * imag, map_real * imag - map_imag * real)
        total = term if total is None else (total[0] + term[0], total[1] + term[1])
    return total


def build_in(flat, flip, get, target, slices):
    outs = flat.shape[2]
    lane = lax.broadcasted_iota(jnp.int32, (outs, target.shape[1]), 1).astype(f32)
    ins = target.shape[1] // (9 * slices)
    lane_slice = jnp.floor((lane + 0.5) * (1.0 / ins))
    lane_slice = lane_slice - slices * jnp.floor((lane_slice + 0.5) * (1.0 / slices))
    wide = []
    for dx in range(3):
        turned = dot_nt(get("eye"), flat[2 - dx if flip else dx].astype(bf16)).astype(bf16)
        wide.append(dot(turned, get("spread")))
    for out_slice in range(slices):
        block = None
        for dx in range(3):
            term = jnp.where(lane_slice == float(out_slice + dx - 1), wide[dx], 0.0)
            block = term if block is None else block + term
        target[out_slice * outs : (out_slice + 1) * outs] = block.astype(bf16)


def build_out(flat, flip, get, target):
    total = None
    for dx in range(3):
        wide = dot(flat[2 - dx if flip else dx].astype(bf16), get("tile")).astype(bf16)
        term = dot(get(("repeat", flip)), wide) * get(("band", dx)).astype(f32)
        total = term if total is None else total + term
    target[...] = total.astype(bf16)


def build_mid(raw, flip, get, target, slices):
    outs, hidden = raw.shape[3], target.shape[0] * target.shape[1]
    out_count, starts, width = groups_of(slices, hidden)
    blocks = []
    for dx in range(3):
        for dy in range(3):
            for dz in range(3):
                if flip:
                    blocks.append(dot_nt(get("eye"), raw[2 - dx, 2 - dy, 2 - dz]))
                else:
                    blocks.append(raw[dx, dy, dz].astype(f32))
    stacked = jnp.concatenate(blocks, axis=0).astype(bf16)
    for index, start in enumerate(starts):
        wide = dot(stacked, get(("mid", index)))
        lane = lax.broadcasted_iota(jnp.int32, (outs, width), 1).astype(f32) + float(start)
        lane_slice = jnp.floor((lane + 0.5) * (1.0 / outs))
        for out_at in range(out_count):
            out_slice = index * out_count + out_at
            keeps = [lane_slice == float(out_slice + dx - 1) for dx in range(3)]
            for tap in range(9):
                block = None
                for dx in range(3):
                    at = (dx * 9 + tap) * outs
                    term = jnp.where(keeps[dx], wide[at : at + outs], 0.0)
                    block = term if block is None else block + term
                target[
                    index, out_at * outs : (out_at + 1) * outs, tap * width : (tap + 1) * width
                ] = block.astype(bf16)


def shifted(values, tap, depth):
    if tap == 1:
        return values
    lane = lax.broadcasted_iota(jnp.int32, (values.shape[0], depth), 1)
    edge, turn = (0, 1) if tap == 0 else (depth - 1, depth - 1)
    pieces = []
    for start in range(0, values.shape[1], depth):
        turned = pltpu.roll(values[:, start : start + depth], turn, 1)
        pieces.append(jnp.where(lane == edge, 0.0, turned))
    return jnp.concatenate(pieces, axis=1)


def conv_in(values, weights, depth):
    width = values.shape[1] - 2 * depth
    turned = [shifted(values, tap, depth) for tap in range(3)]
    stacked = jnp.concatenate(
        [turned[dz][:, dy * depth : dy * depth + width] for dy in range(3) for dz in range(3)],
        axis=0,
    )
    return dot(weights[...], stacked.astype(bf16))


def conv_mid(values, weights, depth, slices):
    cols = values.shape[1] - 2 * depth
    _, starts, width = groups_of(slices, values.shape[0])
    turned = [shifted(values, tap, depth).astype(bf16) for tap in range(3)]
    totals = []
    for index, start in enumerate(starts):
        stacked = jnp.concatenate(
            [
                turned[dz][start : start + width, dy * depth : dy * depth + cols]
                for dy in range(3)
                for dz in range(3)
            ],
            axis=0,
        )
        totals.append(dot(weights[index], stacked))
    return jnp.concatenate(totals, axis=0)


def conv_out(values, weights, depth):
    width = values.shape[1] - 2 * depth
    rows = weights.shape[0] // 9
    products = dot(weights[...], values.astype(bf16))
    total = None
    for dz in range(3):
        summed = None
        for dy in range(3):
            at = (dy * 3 + dz) * rows
            term = products[at : at + rows, dy * depth : dy * depth + width]
            summed = term if summed is None else summed + term
        term = shifted(summed, dz, depth)
        total = term if total is None else total + term
    return total


def sigmoid(values):
    return 0.5 + 0.5 * jnp.tanh(0.5 * values)


def step_kernel(places, *refs):
    (maps_in, kspace_in, mask_in, iterate_in, bits_in, adjoint_in, first_in, second_in,
     last_in, table_in, result, *refs) = refs
    (maps, kspace, mask, iterate, bits, adjoint, raw_first, raw_second, raw_last, table,
     load_sem, *refs) = refs
    (padded, padded_iterate, padded_fields, padded_relaxed, flats, work, rows_work,
     own_iterate, own_fields, all_iterate, halo, parts_send, parts, window_send, windows,
     fields_send, fields, delta_send, delta, grads_send, grads_back, own_pulled, all_pulled,
     sums_send, sums, first, second, last, first_t, second_t, last_t, halo_sem, *sems) = refs
    channels = []
    for index, (axis, how, source, target) in enumerate((
        ("coil", "all", own_iterate, all_iterate),
        ("slab", "row", fields_send, fields),
        ("coil", "row", parts_send, parts),
        ("slab", "row", window_send, windows),
        ("slab", "row", delta_send, delta),
        ("slab", "row", grads_send.at[0], grads_back.at[0]),
        ("slab", "row", grads_send.at[1], grads_back.at[1]),
        ("coil", "all", own_pulled.at[0], all_pulled.at[0]),
        ("coil", "all", own_pulled.at[1], all_pulled.at[1]),
        ("coil", "row", sums_send.at[0], sums.at[0]),
        ("coil", "row", sums_send.at[1], sums.at[1]),
    )):
        channels.append(Channel(axis, how, source, target, sems[2 * index], sems[2 * index + 1]))
    (iterate_way, field_way, part_way, window_way, delta_way, *later) = channels
    grad_ways, pulled_ways, sum_ways = later[:2], later[2:4], later[4:]

    height, depth = mask.shape
    coils, _, rows, _ = all_iterate.shape
    slices, _, window, _ = windows.shape
    own = window - 2 * reach
    block = rows + 2 * reach
    my_coil, my_slab = lax.axis_index("coil"), lax.axis_index("slab")
    row_base = (my_coil * slices + my_slab) * own - reach
    coil_base = pl.multiple_of(my_coil * rows, 8)

    def get(name):
        at, shape = places[name]
        return table[at : at + shape[0], 0 : shape[1]]

    loads = {}
    tables_at = places["ahead"][0]
    for index, (name, source, target) in enumerate((
        ("iterate", iterate_in, iterate),
        ("bits", bits_in, bits),
        ("adjoint", adjoint_in, adjoint),
        ("second", second_in, raw_second),
        ("first", first_in, raw_first),
        ("last", last_in, raw_last),
        ("small", table_in.at[0:tables_at], table.at[0:tables_at]),
        ("maps", maps_in, maps),
        ("tables", table_in.at[tables_at:], table.at[tables_at:]),
        ("mask", mask_in, mask),
        ("kspace", kspace_in, kspace),
    )):
        loads[name] = pltpu.make_async_copy(source, target, load_sem.at[index])
    barrier, arrivals = greet()
    for load in loads.values():
        load.start()
    edge = jnp.zeros((2, 8, depth), f32)
    for target in (padded, padded_iterate):
        target[:, 0:8] = edge
        target[:, height + reach : height + reach + 8] = edge
    loads["iterate"].wait()
    own_iterate[...] = iterate[:, 0].astype(bf16)
    pl.semaphore_wait(barrier, arrivals)
    iterate_way.start()
    loads["bits"].wait()
    loads["adjoint"].wait()
    own_fields[0:2] = (2 * bits[:, 0] - 1).astype(bf16)
    own_fields[2:4] = adjoint[:, 0].astype(bf16)
    halo_ways = []
    for side, (turn, at) in enumerate(((1, rows - 8), (coils - 1, 0))):
        halo_ways.append(
            pltpu.make_async_remote_copy(
                src_ref=own_fields.at[:, at : at + 8],
                dst_ref=halo.at[side],
                send_sem=halo_sem.at[side],
                recv_sem=halo_sem.at[2 + side],
                device_id=place_of("coil", lax.rem(my_coil + turn, coils)),
                device_id_type=MESH,
            )
        )
        halo_ways[-1].start()
    for name in ("second", "first", "last", "small"):
        loads[name].wait()
    for side, raw in enumerate((raw_first, raw_last)):
        for dx in range(3):
            for tap in range(9):
                parts_of = raw[dx, tap // 3, tap % 3].astype(f32)
                flats[2 * side, dx, 2 * tap : 2 * tap + 2] = parts_of
                flats[2 * side + 1, dx, 16 - 2 * tap : 18 - 2 * tap] = parts_of
    build_in(flats.at[3], 1, get, last_t, slices)
    build_in(flats.at[0], 0, get, first, slices)
    build_mid(raw_second, 0, get, second, slices)
    build_mid(raw_second, 1, get, second_t, slices)
    for name in ("maps", "tables", "mask", "kspace"):
        loads[name].wait()
    weight = mask[...].astype(f32)
    all_iterate[my_coil] = own_iterate[...]
    iterate_way.finish()

    def column(gathered, channel):
        return jnp.concatenate(
            [gathered[piece, channel].astype(f32) for piece in range(coils)], axis=0
        )

    real, imag = column(all_iterate, 0), column(all_iterate, 1)
    total = normal_part(real, imag, maps, kspace, weight, get)
    padded[0, reach : reach + height] = total[0]
    padded[1, reach : reach + height] = total[1]
    for piece in range(coils):
        parts_send[piece] = padded[:, piece * rows : piece * rows + block].astype(bf16)
    part_way.start()
    padded_fields[:, reach : reach + rows] = own_fields[...].astype(f32)
    for way in halo_ways:
        way.wait()
    keep = jnp.where(my_coil > 0, 1.0, 0.0).astype(f32)
    padded_fields[:, 0:reach] = halo[0, :, 8 - reach : 8].astype(f32) * keep
    keep = jnp.where(my_coil < coils - 1, 1.0, 0.0).astype(f32)
    padded_fields[:, reach + rows : block] = halo[1, :, 0:reach].astype(f32) * keep
    for piece in range(slices):
        fields_send[piece] = padded_fields[:, piece * own : piece * own + window].astype(bf16)
    field_way.start()
    padded_iterate[0, reach : reach + height] = real
    padded_iterate[1, reach : reach + height] = imag
    padded_relaxed[:, 0:block] = padded_iterate[:, pl.ds(coil_base, block)]
    padded_relaxed[:, reach : reach + rows] = iterate[:, 0]

    def load(values):
        work[...] = values.astype(f32).reshape(work.shape)
        return jnp.concatenate([work[:, row, :] for row in range(window)], axis=1)

    def cut(values, before, after):
        return values[:, before * depth : values.shape[1] - after * depth]

    def inside(values, offset):
        blocks = []
        for row in range(values.shape[1] // depth):
            at = row_base + offset + row
            keep = jnp.where((at >= 0) & (at < height), 1.0, 0.0).astype(f32)
            blocks.append(values[:, row * depth : (row + 1) * depth] * keep)
        return jnp.concatenate(blocks, axis=1)

    def store(values):
        for row in range(own):
            rows_work[:, row, :] = values[:, row * depth : (row + 1) * depth]
        return rows_work[...].reshape(slices, 2, own, depth).astype(bf16)

    build_out(flats.at[2], 0, get, last)
    build_out(flats.at[0], 1, get, first_t)
    part_way.finish()
    summed = padded[:, pl.ds(coil_base, block)]
    for step in range(1, coils):
        summed = summed + parts[lax.rem(my_coil + step, coils)].astype(f32)
    padded_relaxed[:, 0:block] = padded_relaxed[:, 0:block] - step_size * summed
    for piece in range(slices):
        window_send[piece] = padded_relaxed[:, piece * own : piece * own + window].astype(bf16)
    window_way.start()
    windows[my_slab] = window_send[my_slab]
    fields[my_slab] = fields_send[my_slab]
    field_way.finish()
    grads = []
    for field in range(2):
        probe = cut(load(fields[:, 2 * field : 2 * field + 2]), 1, 1)
        grads.append(conv_in(probe, last_t, depth))
    window_way.finish()

    pre1 = conv_in(load(windows[...]), first, depth)
    sig1 = sigmoid(pre1)
    act1 = pre1 * sig1
    slope1 = inside(cut(sig1 + act1 * (1.0 - sig1), 2, 2), 3)
    act1 = inside(act1, 1)
    pre2 = conv_mid(act1, second, depth, slices)
    sig2 = sigmoid(pre2)
    act2 = pre2 * sig2
    slope2 = inside(sig2 + act2 * (1.0 - sig2), 2)
    for field in range(2):
        grad1 = conv_mid(grads[field] * slope2, second_t, depth, slices) * slope1
        grads_send[field] = store(conv_out(grad1, first_t, depth))
        grad_ways[field].start()
        grads_back[field, my_slab] = grads_send[field, my_slab]
    act2 = inside(cut(act2, 1, 1), 3)
    delta_out = store(conv_out(act2, last, depth))

    exact = ((2 * bits[:, 0] - 1).astype(f32), adjoint[:, 0])
    backs = []
    for field in range(2):
        grad_ways[field].finish()
        back = jnp.concatenate(
            [grads_back[field, piece].astype(f32) for piece in range(slices)], axis=1
        )
        backs.append(back)
        own_pulled[field] = (exact[field] + back).astype(bf16)
        pulled_ways[field].start()
        all_pulled[field, my_coil] = own_pulled[field]
        if field == 0:
            delta_send[...] = delta_out
            delta_way.start()
            delta[my_slab] = delta_send[my_slab]
    partial = []
    for field in range(2):
        pulled_ways[field].finish()
        real, imag = column(all_pulled.at[field], 0), column(all_pulled.at[field], 1)
        total = normal_part(real, imag, maps, None, weight, get)
        for part in range(2):
            padded[part, 0:height] = total[part]
            for piece in range(coils):
                sums_send[field, piece, part] = total[part][
                    piece * rows : (piece + 1) * rows
                ].astype(bf16)
        sum_ways[field].start()
        partial.append(padded[:, pl.ds(coil_base, rows)])

    delta_way.finish()
    for piece in range(slices):
        at = piece * own
        result[0, :, at : at + own] = (
            padded_relaxed[:, reach + at : reach + at + own] - iterate[:, 0, at : at + own]
        ) + delta[piece].astype(f32)
    for field in range(2):
        sum_ways[field].finish()
        added = partial[field]
        for step in range(1, coils):
            added = added + sums[field, lax.rem(my_coil + step, coils)].astype(f32)
        result[1 + field] = backs[field] - step_size * added


def on_device(coil_maps, kspace, sample_mask, iterate, probe_bits, loss_gradient, adjoint,
              kernel_first, kernel_second, kernel_last):
    height, depth = sample_mask.shape
    coils, slabs = lax.axis_size("coil"), lax.axis_size("slab")
    own = height // (coils * slabs)
    window = own + 2 * reach
    rows = iterate.shape[2]
    block = rows + 2 * reach
    hidden, channels = kernel_second.shape[0] * slabs, kernel_first.shape[1] * slabs
    table, places = pack_constants(height, depth, slabs, hidden, channels)
    raws = (
        jnp.transpose(kernel_first, (2, 3, 4, 1, 0)),
        jnp.transpose(kernel_second, (2, 3, 4, 0, 1)),
        jnp.transpose(kernel_last, (2, 3, 4, 0, 1)),
    )
    operands = (coil_maps, kspace, sample_mask, iterate, probe_bits, adjoint, *raws,
                jnp.asarray(table))
    _, starts, width = groups_of(slabs, hidden)
    mids = (len(starts), hidden // len(starts), 9 * width)
    buffers = [
        ((2, height + 2 * reach + 8, depth), f32),
        ((2, height + 2 * reach + 8, depth), f32),
        ((4, block + 8, depth), f32),
        ((2, block + 8, depth), f32),
        ((4, 3, 18, kernel_second.shape[0]), f32),
        ((2 * slabs, window, depth), f32),
        ((2 * slabs, own, depth), f32),
        ((2, rows, depth), bf16),
        ((4, rows, depth), bf16),
        ((coils, 2, rows, depth), bf16),
        ((2, 4, 8, depth), bf16),
        ((coils, 2, block, depth), bf16),
        ((coils, 2, block, depth), bf16),
        ((slabs, 2, window, depth), bf16),
        ((slabs, 2, window, depth), bf16),
        ((slabs, 4, window, depth), bf16),
        ((slabs, 4, window, depth), bf16),
        ((slabs, 2, own, depth), bf16),
        ((slabs, 2, own, depth), bf16),
        ((2, slabs, 2, own, depth), bf16),
        ((2, slabs, 2, own, depth), bf16),
        ((2, 2, rows, depth), bf16),
        ((2, coils, 2, rows, depth), bf16),
        ((2, coils, 2, rows, depth), bf16),
        ((2, coils, 2, rows, depth), bf16),
        ((hidden, 9 * channels), bf16),
        (mids, bf16),
        ((9 * channels, hidden), bf16),
        ((9 * channels, hidden), bf16),
        (mids, bf16),
        ((hidden, 9 * channels), bf16),
    ]
    changes = pl.pallas_call(
        lambda *refs: step_kernel(places, *refs),
        out_shape=pltpu.VMEM((3, 2, rows, depth), f32),
        in_specs=[in_hbm] * len(operands),
        out_specs=in_vmem,
        scratch_shapes=[pltpu.VMEM(value.shape, value.dtype) for value in operands]
        + [pltpu.SemaphoreType.DMA((11,))]
        + [pltpu.VMEM(shape, kind) for shape, kind in buffers]
        + [pltpu.SemaphoreType.DMA((4,))]
        + [pltpu.SemaphoreType.DMA] * 22,
        compiler_params=pltpu.CompilerParams(
            collective_id=0, has_side_effects=True, vmem_limit_bytes=40 << 20
        ),
        name="step",
    )(*[pltpu.with_memory_space_constraint(value, pltpu.HBM) for value in operands])
    changes = changes[:, :, None]
    sign = (2 * probe_bits - 1).astype(f32)
    return iterate + changes[0], sign + changes[1], loss_gradient + (adjoint + changes[2])


def solution(mesh):
    split_coils = P("coil", None, "slab", None, None)
    image = P(None, "slab", "coil", None)
    return jax.shard_map(
        on_device,
        mesh=mesh,
        in_specs=(split_coils, split_coils, P(), image, image, image, image, P(), P(), P()),
        out_specs=(image, image, image),
        check_vma=False,
    )
```

```python
import jax
import jax.numpy as jnp
import numpy as np
from jax import lax
from jax.experimental import pallas as pl
from jax.experimental.pallas import tpu as pltpu
from jax.sharding import PartitionSpec as P

step_size = 0.8
reach = 4
f32 = jnp.float32
bf16 = jnp.bfloat16
in_hbm = pl.BlockSpec(memory_space=pltpu.HBM)
in_vmem = pl.BlockSpec(memory_space=pltpu.VMEM)
MESH = pl.DeviceIdType.MESH


class Channel:
    def __init__(self, axis, how, source, target, send_sem, recv_sem):
        self.axis, self.how, self.source, self.target = axis, how, source, target
        self.send_sem, self.recv_sem = send_sem, recv_sem
        self.size, self.mine = lax.axis_size(axis), lax.axis_index(axis)

    def row(self, rank):
        return self.source if self.how == "all" else self.source.at[rank]

    def copy(self, source_rank, target_row, device_rank):
        return pltpu.make_async_remote_copy(
            src_ref=self.row(source_rank),
            dst_ref=self.target.at[target_row],
            send_sem=self.send_sem,
            recv_sem=self.recv_sem,
            device_id=place_of(self.axis, device_rank),
            device_id_type=MESH,
        )

    def start(self):
        for step in range(1, self.size):
            rank = lax.rem(self.mine + step, self.size)
            self.copy(rank, self.mine, rank).start()

    def finish(self):
        landed = self.target.at[0 : self.size - 1]
        for sem in (self.send_sem, self.recv_sem):
            pltpu.make_async_copy(landed, landed, sem).wait()


def place_of(axis, rank):
    if axis == "coil":
        return rank, lax.axis_index("slab")
    return lax.axis_index("coil"), rank


def greet():
    barrier = pltpu.get_barrier_semaphore()
    count = 0
    for axis in ("coil", "slab"):
        size = lax.axis_size(axis)
        for step in range(1, size):
            rank = lax.rem(lax.axis_index(axis) + step, size)
            pl.semaphore_signal(
                barrier, inc=1, device_id=place_of(axis, rank), device_id_type=MESH
            )
            count += 1
    return barrier, count


def high_low(table):
    high = np.asarray(table, np.float32).astype(jnp.bfloat16)
    return high, (np.asarray(table, np.float32) - high.astype(np.float32)).astype(jnp.bfloat16)


def fourier_tables(height, depth):
    def parts(length):
        counter = np.arange(length)
        angles = (counter[:, None] * counter[None, :] % length) * (2.0 * np.pi / length)
        return np.cos(angles) / np.sqrt(length), np.sin(angles) / np.sqrt(length)

    cos, sin = parts(depth)
    forward = np.block([[cos, -sin], [sin, cos]])
    backward = np.block([[cos, sin], [-sin, cos]])
    return high_low(forward) + high_low(backward) + high_low(np.concatenate(parts(height)))


def groups_of(slices, hidden):
    per = hidden // slices
    out = 4 if slices % 4 == 0 else slices
    spans = []
    for first in range(0, slices, out):
        low = max(first - 1, 0) * per // 32 * 32
        high = min(first + out + 1, slices) * per
        spans.append((low, high))
    width = -(-max(high - low for low, high in spans) // 128) * 128
    if width >= hidden:
        return slices, [0], hidden
    return out, [min(low, hidden - width) for low, _ in spans], width


def mid_eye(hidden, slices, start, width):
    lanes = start + np.arange(width)
    return np.arange(hidden // slices)[:, None] == lanes[None, :] % (hidden // slices)


def pack_constants(height, depth, slices, hidden, channels):
    outs, ins = hidden // slices, channels // slices
    _, starts, width = groups_of(slices, hidden)
    taps = 9
    rows = np.arange(taps * slices * ins)
    row_slice, row_part, row_tap = rows // ins % slices, rows % ins, rows // (slices * ins)
    lane_slice = np.arange(hidden) // outs
    items = {
        "eye": np.eye(outs),
        "spread": np.kron(np.eye(taps), np.tile(np.eye(ins), (1, slices))),
        "tile": np.tile(np.eye(outs), (1, slices)),
    }
    for index, start in enumerate(starts):
        items["mid", index] = mid_eye(hidden, slices, start, width)
    for flip in range(2):
        tap = taps - 1 - row_tap if flip else row_tap
        items["repeat", flip] = (
            np.arange(taps * ins)[None, :] == (tap * ins + row_part)[:, None]
        )
    for dx in range(3):
        items["band", dx] = lane_slice[None, :] == row_slice[:, None] + dx - 1
    names = ("ahead", "ahead_low", "back", "back_low", "down", "down_low")
    items.update(zip(names, fourier_tables(height, depth)))
    lanes = -(-max(item.shape[1] for item in items.values()) // 128) * 128
    places, blocks, at = {}, [], 0
    for name, item in items.items():
        count = -(-item.shape[0] // 16) * 16
        block = np.zeros((count, lanes), jnp.bfloat16)
        block[: item.shape[0], : item.shape[1]] = np.asarray(item).astype(jnp.bfloat16)
        places[name] = (at, item.shape)
        blocks.append(block)
        at += count
    return np.concatenate(blocks), places


def dot(left, right):
    return jnp.dot(left, right, preferred_element_type=f32)


def dot_nt(left, right):
    return lax.dot_general(left, right, (((1,), (1,)), ((), ())), preferred_element_type=f32)


def halves(values):
    high = values.astype(bf16)
    return high, (values - high.astype(f32)).astype(bf16)


def spectrum(images, get, inverse, fine):
    count, height, depth = len(images), images[0].shape[0], images[0].shape[1] // 2
    names = ("back", "back_low") if inverse else ("ahead", "ahead_low")
    high, low = halves(jnp.concatenate(images, axis=0))
    turned = dot(high, get(names[0]))
    if fine:
        turned = turned + (dot(low, get(names[0])) + dot(high, get(names[1])))
    turned = jnp.concatenate(
        [turned[at * height : (at + 1) * height] for at in range(count)], axis=1
    )
    high = turned.astype(bf16)
    both_parts = dot(get("down"), high)
    results = []
    for at in range(count):
        start = 2 * at * depth
        upper = both_parts[:height, start : start + 2 * depth]
        lower = both_parts[height:, start : start + 2 * depth]
        if inverse:
            results.append(
                (upper[:, :depth] - lower[:, depth:], lower[:, :depth] + upper[:, depth:])
            )
        else:
            results.append(
                (upper[:, :depth] + lower[:, depth:], upper[:, depth:] - lower[:, :depth])
            )
    return results


def normal_part(real, imag, maps, kspace, mask, get):
    images = []
    for coil in range(maps.shape[0]):
        map_real, map_imag = maps[coil, 0, 0], maps[coil, 1, 0]
        images.append(
            jnp.concatenate(
                [map_real * real - map_imag * imag, map_real * imag + map_imag * real], axis=1
            )
        )
    masked = []
    for coil, (freq_real, freq_imag) in enumerate(spectrum(images, get, False, False)):
        if kspace is not None:
            freq_real = freq_real - kspace[coil, 0, 0]
            freq_imag = freq_imag - kspace[coil, 1, 0]
        masked.append(jnp.concatenate([mask * freq_real, mask * freq_imag], axis=1))
    total = None
    for coil, (real, imag) in enumerate(spectrum(masked, get, True, kspace is not None)):
        map_real, map_imag = maps[coil, 0, 0], maps[coil, 1, 0]
        term = (map_real * real + map_imag * imag, map_real * imag - map_imag * real)
        total = term if total is None else (total[0] + term[0], total[1] + term[1])
    return total


def build_in(flat, flip, get, target, slices):
    outs = flat.shape[2]
    lane = lax.broadcasted_iota(jnp.int32, (outs, target.shape[1]), 1).astype(f32)
    ins = target.shape[1] // (9 * slices)
    lane_slice = jnp.floor((lane + 0.5) * (1.0 / ins))
    lane_slice = lane_slice - slices * jnp.floor((lane_slice + 0.5) * (1.0 / slices))
    wide = []
    for dx in range(3):
        turned = dot_nt(get("eye"), flat[2 - dx if flip else dx].astype(bf16)).astype(bf16)
        wide.append(dot(turned, get("spread")))
    for out_slice in range(slices):
        block = None
        for dx in range(3):
            term = jnp.where(lane_slice == float(out_slice + dx - 1), wide[dx], 0.0)
            block = term if block is None else block + term
        target[out_slice * outs : (out_slice + 1) * outs] = block.astype(bf16)


def build_out(flat, flip, get, target):
    total = None
    for dx in range(3):
        wide = dot(flat[2 - dx if flip else dx].astype(bf16), get("tile")).astype(bf16)
        term = dot(get(("repeat", flip)), wide) * get(("band", dx)).astype(f32)
        total = term if total is None else total + term
    target[...] = total.astype(bf16)


def build_mid(raw, flip, get, target, slices):
    outs = raw.shape[3]
    hidden = outs * slices
    out_count, starts, width = groups_of(slices, hidden)
    blocks = []
    for dx in range(3):
        for dy in range(3):
            for dz in range(3):
                if flip:
                    blocks.append(dot_nt(get("eye"), raw[2 - dx, 2 - dy, 2 - dz]))
                else:
                    blocks.append(raw[dx, dy, dz].astype(f32))
    stacked = jnp.concatenate(blocks, axis=0).astype(bf16)
    for index, start in enumerate(starts):
        wide = dot(stacked, get(("mid", index)))
        lane = lax.broadcasted_iota(jnp.int32, (outs, width), 1).astype(f32) + float(start)
        lane_slice = jnp.floor((lane + 0.5) * (1.0 / outs))
        for out_at in range(out_count):
            out_slice = index * out_count + out_at
            keeps = [lane_slice == float(out_slice + dx - 1) for dx in range(3)]
            for tap in range(9):
                block = None
                for dx in range(3):
                    at = (dx * 9 + tap) * outs
                    term = jnp.where(keeps[dx], wide[at : at + outs], 0.0)
                    block = term if block is None else block + term
                at = (tap % 3 * out_count + out_at) * outs
                target[
                    index, at : at + outs, tap // 3 * width : (tap // 3 + 1) * width
                ] = block.astype(bf16)


def shifted(values, tap, depth):
    if tap == 1:
        return values
    lane = lax.broadcasted_iota(jnp.int32, (values.shape[0], depth), 1)
    edge, turn = (0, 1) if tap == 0 else (depth - 1, depth - 1)
    pieces = []
    for start in range(0, values.shape[1], depth):
        turned = pltpu.roll(values[:, start : start + depth], turn, 1)
        pieces.append(jnp.where(lane == edge, 0.0, turned))
    return jnp.concatenate(pieces, axis=1)


def conv_in(values, weights, depth):
    width = values.shape[1] - 2 * depth
    turned = [shifted(values, tap, depth) for tap in range(3)]
    stacked = jnp.concatenate(
        [turned[dz][:, dy * depth : dy * depth + width] for dy in range(3) for dz in range(3)],
        axis=0,
    )
    return dot(weights[...], stacked.astype(bf16))


def conv_mid(values, weights, depth, slices):
    cols = values.shape[1] - 2 * depth
    _, starts, width = groups_of(slices, values.shape[0])
    held = values.astype(bf16)
    totals = []
    for index, start in enumerate(starts):
        stacked = jnp.concatenate(
            [held[start : start + width, dy * depth : dy * depth + cols] for dy in range(3)],
            axis=0,
        )
        products = dot(weights[index], stacked)
        rows = products.shape[0] // 3
        total = products[rows : 2 * rows]
        for dz in (0, 2):
            total = total + shifted(products[dz * rows : (dz + 1) * rows], dz, depth)
        totals.append(total)
    return jnp.concatenate(totals, axis=0)


def conv_out(values, weights, depth):
    width = values.shape[1] - 2 * depth
    rows = weights.shape[0] // 9
    products = dot(weights[...], values.astype(bf16))
    total = None
    for dz in range(3):
        summed = None
        for dy in range(3):
            at = (dy * 3 + dz) * rows
            term = products[at : at + rows, dy * depth : dy * depth + width]
            summed = term if summed is None else summed + term
        term = shifted(summed, dz, depth)
        total = term if total is None else total + term
    return total


def sigmoid(values):
    return 0.5 + 0.5 * jnp.tanh(0.5 * values)


def step_kernel(places, *refs):
    (maps_in, kspace_in, mask_in, iterate_in, bits_in, adjoint_in, first_in, second_in,
     last_in, table_in, result, *refs) = refs
    (maps, kspace, mask, iterate, bits, adjoint, raw_first, raw_second, raw_last, table,
     load_sem, *refs) = refs
    (padded, padded_iterate, padded_fields, padded_relaxed, flats, work, rows_work,
     own_iterate, own_fields, all_iterate, halo, parts_send, parts, window_send, windows,
     fields_send, fields, delta_send, delta, grads_send, grads_back, own_pulled, all_pulled,
     sums_send, sums, first, second, last, first_t, second_t, last_t, exact, halo_sem, back_send,
     back_recv, pulled_send, pulled_recv, *sems) = refs
    channels = []
    for index, (axis, how, source, target) in enumerate((
        ("coil", "all", own_iterate, all_iterate),
        ("slab", "row", fields_send, fields),
        ("coil", "row", parts_send, parts),
        ("slab", "row", window_send, windows),
        ("slab", "row", delta_send, delta),
        ("coil", "row", sums_send.at[0], sums.at[0]),
        ("coil", "row", sums_send.at[1], sums.at[1]),
    )):
        channels.append(Channel(axis, how, source, target, sems[2 * index], sems[2 * index + 1]))
    (iterate_way, field_way, part_way, window_way, delta_way, *later) = channels
    sum_ways = later

    height, depth = mask.shape
    coils, _, rows, _ = all_iterate.shape
    slices, _, window, _ = windows.shape
    own = window - 2 * reach
    block = rows + 2 * reach
    my_coil, my_slab = lax.axis_index("coil"), lax.axis_index("slab")
    row_base = (my_coil * slices + my_slab) * own - reach
    coil_base = pl.multiple_of(my_coil * rows, 8)

    def get(name):
        at, shape = places[name]
        return table[at : at + shape[0], 0 : shape[1]]

    loads = {}
    tables_at = places["ahead"][0]
    for index, (name, source, target) in enumerate((
        ("iterate", iterate_in, iterate),
        ("bits", bits_in, bits),
        ("adjoint", adjoint_in, adjoint),
        ("second", second_in, raw_second),
        ("first", first_in, raw_first),
        ("last", last_in, raw_last),
        ("small", table_in.at[0:tables_at], table.at[0:tables_at]),
        ("maps", maps_in, maps),
        ("tables", table_in.at[tables_at:], table.at[tables_at:]),
        ("mask", mask_in, mask),
        ("kspace", kspace_in, kspace),
    )):
        loads[name] = pltpu.make_async_copy(source, target, load_sem.at[index])
    barrier, arrivals = greet()
    for load in loads.values():
        load.start()
    edge = jnp.zeros((2, 8, depth), f32)
    for target in (padded, padded_iterate):
        target[:, 0:8] = edge
        target[:, height + reach : height + reach + 8] = edge
    loads["iterate"].wait()
    own_iterate[...] = iterate[:, 0].astype(bf16)
    pl.semaphore_wait(barrier, arrivals)
    iterate_way.start()
    loads["bits"].wait()
    loads["adjoint"].wait()
    own_fields[0:2] = (2 * bits[:, 0] - 1).astype(bf16)
    own_fields[2:4] = adjoint[:, 0].astype(bf16)
    halo_ways = []
    for side, (turn, at) in enumerate(((1, rows - 8), (coils - 1, 0))):
        halo_ways.append(
            pltpu.make_async_remote_copy(
                src_ref=own_fields.at[:, at : at + 8],
                dst_ref=halo.at[side],
                send_sem=halo_sem.at[side],
                recv_sem=halo_sem.at[2 + side],
                device_id=place_of("coil", lax.rem(my_coil + turn, coils)),
                device_id_type=MESH,
            )
        )
        halo_ways[-1].start()
    for name in ("second", "first", "last", "small"):
        loads[name].wait()
    for side, raw in enumerate((raw_first, raw_last)):
        for dx in range(3):
            for tap in range(9):
                parts_of = raw[dx, tap // 3, tap % 3].astype(f32)
                flats[2 * side, dx, 2 * tap : 2 * tap + 2] = parts_of
                flats[2 * side + 1, dx, 16 - 2 * tap : 18 - 2 * tap] = parts_of
    build_in(flats.at[3], 1, get, last_t, slices)
    build_in(flats.at[0], 0, get, first, slices)
    build_mid(raw_second, 0, get, second, slices)
    build_mid(raw_second, 1, get, second_t, slices)
    for name in ("maps", "tables", "mask", "kspace"):
        loads[name].wait()
    weight = mask[...].astype(f32)
    all_iterate[my_coil] = own_iterate[...]
    iterate_way.finish()

    def column(gathered, channel):
        return jnp.concatenate(
            [gathered[piece, channel].astype(f32) for piece in range(coils)], axis=0
        )

    real, imag = column(all_iterate, 0), column(all_iterate, 1)
    total = normal_part(real, imag, maps, kspace, weight, get)
    padded[0, reach : reach + height] = total[0]
    padded[1, reach : reach + height] = total[1]
    for piece in range(coils):
        parts_send[piece] = padded[:, piece * rows : piece * rows + block].astype(bf16)
    part_way.start()
    padded_fields[:, reach : reach + rows] = own_fields[...].astype(f32)
    for way in halo_ways:
        way.wait()
    keep = jnp.where(my_coil > 0, 1.0, 0.0).astype(f32)
    padded_fields[:, 0:reach] = halo[0, :, 8 - reach : 8].astype(f32) * keep
    keep = jnp.where(my_coil < coils - 1, 1.0, 0.0).astype(f32)
    padded_fields[:, reach + rows : block] = halo[1, :, 0:reach].astype(f32) * keep
    for piece in range(slices):
        fields_send[piece] = padded_fields[:, piece * own : piece * own + window].astype(bf16)
    field_way.start()
    padded_iterate[0, reach : reach + height] = real
    padded_iterate[1, reach : reach + height] = imag
    padded_relaxed[:, 0:block] = padded_iterate[:, pl.ds(coil_base, block)]
    padded_relaxed[:, reach : reach + rows] = iterate[:, 0]

    def load(values):
        work[...] = values.astype(f32).reshape(work.shape)
        return jnp.concatenate([work[:, row, :] for row in range(window)], axis=1)

    def cut(values, before, after):
        return values[:, before * depth : values.shape[1] - after * depth]

    def inside(values, offset):
        blocks = []
        for row in range(values.shape[1] // depth):
            at = row_base + offset + row
            keep = jnp.where((at >= 0) & (at < height), 1.0, 0.0).astype(f32)
            blocks.append(values[:, row * depth : (row + 1) * depth] * keep)
        return jnp.concatenate(blocks, axis=1)

    def store(values):
        for row in range(own):
            rows_work[:, row, :] = values[:, row * depth : (row + 1) * depth]
        return rows_work[...].reshape(slices, 2, own, depth).astype(bf16)

    build_out(flats.at[2], 0, get, last)
    build_out(flats.at[0], 1, get, first_t)
    part_way.finish()
    summed = padded[:, pl.ds(coil_base, block)]
    for step in range(1, coils):
        summed = summed + parts[lax.rem(my_coil + step, coils)].astype(f32)
    padded_relaxed[:, 0:block] = padded_relaxed[:, 0:block] - step_size * summed
    for piece in range(slices):
        window_send[piece] = padded_relaxed[:, piece * own : piece * own + window].astype(bf16)
    window_way.start()
    windows[my_slab] = window_send[my_slab]
    pair = 2 if slices % 2 == 0 else 1
    groups = slices // pair
    my_group = lax.div(my_slab, pair)

    def send_back(field):
        for step in range(1, slices):
            rank = lax.rem(my_slab + step, slices)
            group = lax.rem(my_group + groups - lax.div(rank, pair), groups)
            pltpu.make_async_remote_copy(
                src_ref=grads_send.at[field, rank],
                dst_ref=grads_back.at[field, my_slab],
                send_sem=back_send.at[field],
                recv_sem=back_recv.at[field, group],
                device_id=place_of("slab", rank),
                device_id_type=MESH,
            ).start()

    def pass_on(field):
        for step in range(groups):
            count = pair if step else pair - 1
            group = lax.rem(my_group + step, groups)
            if count:
                landed = grads_back.at[field, 0:count]
                pltpu.make_async_copy(landed, landed, back_recv.at[field, step]).wait()
            for index in range(pair):
                piece = group * pair + index
                own_pulled[field, piece] = (
                    exact[field, piece] + grads_back[field, piece].astype(f32)
                ).astype(bf16)
            span = pl.ds(group * pair, pair)
            for turn in range(1, coils):
                pltpu.make_async_remote_copy(
                    src_ref=own_pulled.at[field, span],
                    dst_ref=all_pulled.at[field, my_coil, span],
                    send_sem=pulled_send.at[field],
                    recv_sem=pulled_recv.at[field],
                    device_id=place_of("coil", lax.rem(my_coil + turn, coils)),
                    device_id_type=MESH,
                ).start()
        all_pulled[field, my_coil] = own_pulled[field]

    for piece in range(slices):
        at = slice(piece * own, (piece + 1) * own)
        exact[0, piece] = (2 * bits[:, 0, at] - 1).astype(f32)
        exact[1, piece] = adjoint[:, 0, at]
    fields[my_slab] = fields_send[my_slab]
    field_way.finish()
    grads = []
    for field in range(2):
        probe = cut(load(fields[:, 2 * field : 2 * field + 2]), 1, 1)
        grads.append(conv_in(probe, last_t, depth))
    window_way.finish()

    pre1 = conv_in(load(windows[...]), first, depth)
    sig1 = sigmoid(pre1)
    act1 = pre1 * sig1
    slope1 = inside(cut(sig1 + act1 * (1.0 - sig1), 2, 2), 3)
    act1 = inside(act1, 1)
    pre2 = conv_mid(act1, second, depth, slices)
    sig2 = sigmoid(pre2)
    act2 = pre2 * sig2
    slope2 = inside(sig2 + act2 * (1.0 - sig2), 2)
    for field in range(2):
        grad1 = conv_mid(grads[field] * slope2, second_t, depth, slices) * slope1
        grads_send[field] = store(conv_out(grad1, first_t, depth))
        send_back(field)
        grads_back[field, my_slab] = grads_send[field, my_slab]
    act2 = inside(cut(act2, 1, 1), 3)
    delta_out = store(conv_out(act2, last, depth))

    for field in range(2):
        pass_on(field)
        if field == 0:
            delta_send[...] = delta_out
            delta_way.start()
            delta[my_slab] = delta_send[my_slab]
    partial = []
    for field in range(2):
        landed = all_pulled.at[field, 0 : coils - 1]
        for sem in (pulled_send, pulled_recv):
            pltpu.make_async_copy(landed, landed, sem.at[field]).wait()
        real, imag = (
            jnp.concatenate(
                [
                    all_pulled[field, piece // slices, piece % slices, part].astype(f32)
                    for piece in range(coils * slices)
                ],
                axis=0,
            )
            for part in range(2)
        )
        total = normal_part(real, imag, maps, None, weight, get)
        for part in range(2):
            padded[part, 0:height] = total[part]
            for piece in range(coils):
                sums_send[field, piece, part] = total[part][
                    piece * rows : (piece + 1) * rows
                ].astype(bf16)
        sum_ways[field].start()
        partial.append(padded[:, pl.ds(coil_base, rows)])

    backs = []
    for field in range(2):
        landed = grads_back.at[field, 0 : slices - 1]
        pltpu.make_async_copy(landed, landed, back_send.at[field]).wait()
        backs.append(
            jnp.concatenate(
                [grads_back[field, piece].astype(f32) for piece in range(slices)], axis=1
            )
        )
    delta_way.finish()
    for piece in range(slices):
        at = piece * own
        result[0, :, at : at + own] = (
            padded_relaxed[:, reach + at : reach + at + own] - iterate[:, 0, at : at + own]
        ) + delta[piece].astype(f32)
    for field in range(2):
        sum_ways[field].finish()
        added = partial[field]
        for step in range(1, coils):
            added = added + sums[field, lax.rem(my_coil + step, coils)].astype(f32)
        result[1 + field] = backs[field] - step_size * added


def on_device(coil_maps, kspace, sample_mask, iterate, probe_bits, loss_gradient, adjoint,
              kernel_first, kernel_second, kernel_last):
    height, depth = sample_mask.shape
    coils, slabs = lax.axis_size("coil"), lax.axis_size("slab")
    own = height // (coils * slabs)
    window = own + 2 * reach
    rows = iterate.shape[2]
    block = rows + 2 * reach
    hidden, channels = kernel_second.shape[0] * slabs, kernel_first.shape[1] * slabs
    table, places = pack_constants(height, depth, slabs, hidden, channels)
    raws = (
        jnp.transpose(kernel_first, (2, 3, 4, 1, 0)),
        jnp.transpose(kernel_second, (2, 3, 4, 0, 1)),
        jnp.transpose(kernel_last, (2, 3, 4, 0, 1)),
    )
    operands = (coil_maps, kspace, sample_mask, iterate, probe_bits, adjoint, *raws,
                jnp.asarray(table))
    _, starts, width = groups_of(slabs, hidden)
    mids = (len(starts), 3 * hidden // len(starts), 3 * width)
    buffers = [
        ((2, height + 2 * reach + 8, depth), f32),
        ((2, height + 2 * reach + 8, depth), f32),
        ((4, block + 8, depth), f32),
        ((2, block + 8, depth), f32),
        ((4, 3, 18, kernel_second.shape[0]), f32),
        ((2 * slabs, window, depth), f32),
        ((2 * slabs, own, depth), f32),
        ((2, rows, depth), bf16),
        ((4, rows, depth), bf16),
        ((coils, 2, rows, depth), bf16),
        ((2, 4, 8, depth), bf16),
        ((coils, 2, block, depth), bf16),
        ((coils, 2, block, depth), bf16),
        ((slabs, 2, window, depth), bf16),
        ((slabs, 2, window, depth), bf16),
        ((slabs, 4, window, depth), bf16),
        ((slabs, 4, window, depth), bf16),
        ((slabs, 2, own, depth), bf16),
        ((slabs, 2, own, depth), bf16),
        ((2, slabs, 2, own, depth), bf16),
        ((2, slabs, 2, own, depth), bf16),
        ((2, slabs, 2, own, depth), bf16),
        ((2, coils, slabs, 2, own, depth), bf16),
        ((2, coils, 2, rows, depth), bf16),
        ((2, coils, 2, rows, depth), bf16),
        ((hidden, 9 * channels), bf16),
        (mids, bf16),
        ((9 * channels, hidden), bf16),
        ((9 * channels, hidden), bf16),
        (mids, bf16),
        ((hidden, 9 * channels), bf16),
        ((2, slabs, 2, own, depth), f32),
    ]
    groups = slabs // 2 if slabs % 2 == 0 else slabs
    changes = pl.pallas_call(
        lambda *refs: step_kernel(places, *refs),
        out_shape=pltpu.VMEM((3, 2, rows, depth), f32),
        in_specs=[in_hbm] * len(operands),
        out_specs=in_vmem,
        scratch_shapes=[pltpu.VMEM(value.shape, value.dtype) for value in operands]
        + [pltpu.SemaphoreType.DMA((11,))]
        + [pltpu.VMEM(shape, kind) for shape, kind in buffers]
        + [pltpu.SemaphoreType.DMA((4,))]
        + [pltpu.SemaphoreType.DMA((2,)), pltpu.SemaphoreType.DMA((2, groups))]
        + [pltpu.SemaphoreType.DMA((2,))] * 2
        + [pltpu.SemaphoreType.DMA] * 14,
        compiler_params=pltpu.CompilerParams(
            collective_id=0, has_side_effects=True, vmem_limit_bytes=40 << 20
        ),
        name="step",
    )(*[pltpu.with_memory_space_constraint(value, pltpu.HBM) for value in operands])
    changes = changes[:, :, None]
    sign = (2 * probe_bits - 1).astype(f32)
    return iterate + changes[0], sign + changes[1], loss_gradient + (adjoint + changes[2])


def solution(mesh):
    split_coils = P("coil", None, "slab", None, None)
    image = P(None, "slab", "coil", None)
    return jax.shard_map(
        on_device,
        mesh=mesh,
        in_specs=(split_coils, split_coils, P(), image, image, image, image, P(), P(), P()),
        out_specs=(image, image, image),
        check_vma=False,
    )
```

```python
import jax
import jax.numpy as jnp
import numpy as np
from jax import lax
from jax.experimental import pallas as pl
from jax.experimental.pallas import tpu as pltpu
from jax.sharding import PartitionSpec as P

step_size = 0.8
reach = 4
f32 = jnp.float32
bf16 = jnp.bfloat16
in_hbm = pl.BlockSpec(memory_space=pltpu.HBM)
in_vmem = pl.BlockSpec(memory_space=pltpu.VMEM)
MESH = pl.DeviceIdType.MESH


class Channel:
    def __init__(self, axis, how, source, target, send_sem, recv_sem):
        self.axis, self.how, self.source, self.target = axis, how, source, target
        self.send_sem, self.recv_sem = send_sem, recv_sem
        self.size, self.mine = lax.axis_size(axis), lax.axis_index(axis)

    def row(self, rank):
        return self.source if self.how == "all" else self.source.at[rank]

    def copy(self, source_rank, target_row, device_rank):
        return pltpu.make_async_remote_copy(
            src_ref=self.row(source_rank),
            dst_ref=self.target.at[target_row],
            send_sem=self.send_sem,
            recv_sem=self.recv_sem,
            device_id=place_of(self.axis, device_rank),
            device_id_type=MESH,
        )

    def start(self):
        for step in far_first(self.size):
            rank = lax.rem(self.mine + step, self.size)
            self.copy(rank, self.mine, rank).start()

    def finish(self):
        landed = self.target.at[0 : self.size - 1]
        for sem in (self.send_sem, self.recv_sem):
            pltpu.make_async_copy(landed, landed, sem).wait()


def far_first(size):
    return sorted(range(1, size), key=lambda step: abs(2 * step - size))


def place_of(axis, rank):
    if axis == "coil":
        return rank, lax.axis_index("slab")
    return lax.axis_index("coil"), rank


def greet():
    barrier = pltpu.get_barrier_semaphore()
    count = 0
    for axis in ("coil", "slab"):
        size = lax.axis_size(axis)
        for step in range(1, size):
            rank = lax.rem(lax.axis_index(axis) + step, size)
            pl.semaphore_signal(
                barrier, inc=1, device_id=place_of(axis, rank), device_id_type=MESH
            )
            count += 1
    return barrier, count


def high_low(table):
    high = np.asarray(table, np.float32).astype(jnp.bfloat16)
    return high, (np.asarray(table, np.float32) - high.astype(np.float32)).astype(jnp.bfloat16)


def fourier_tables(height, depth):
    def parts(length):
        counter = np.arange(length)
        angles = (counter[:, None] * counter[None, :] % length) * (2.0 * np.pi / length)
        return np.cos(angles) / np.sqrt(length), np.sin(angles) / np.sqrt(length)

    cos, sin = parts(depth)
    forward = np.block([[cos, -sin], [sin, cos]])
    backward = np.block([[cos, sin], [-sin, cos]])
    return high_low(forward) + high_low(backward) + high_low(np.concatenate(parts(height)))


def groups_of(slices, hidden):
    per = hidden // slices
    out = 4 if slices % 4 == 0 else slices
    spans = []
    for first in range(0, slices, out):
        low = max(first - 1, 0) * per // 32 * 32
        high = min(first + out + 1, slices) * per
        spans.append((low, high))
    width = -(-max(high - low for low, high in spans) // 128) * 128
    if width >= hidden:
        return slices, [0], hidden
    return out, [min(low, hidden - width) for low, _ in spans], width


def mid_eye(hidden, slices, start, width):
    lanes = start + np.arange(width)
    return np.arange(hidden // slices)[:, None] == lanes[None, :] % (hidden // slices)


def pack_constants(height, depth, slices, hidden, channels):
    outs, ins = hidden // slices, channels // slices
    _, starts, width = groups_of(slices, hidden)
    taps = 9
    rows = np.arange(taps * slices * ins)
    row_slice, row_part, row_tap = rows // ins % slices, rows % ins, rows // (slices * ins)
    lane_slice = np.arange(hidden) // outs
    items = {
        "eye": np.eye(outs),
        "spread": np.kron(np.eye(taps), np.tile(np.eye(ins), (1, slices))),
        "tile": np.tile(np.eye(outs), (1, slices)),
    }
    for index, start in enumerate(starts):
        items["mid", index] = mid_eye(hidden, slices, start, width)
    for flip in range(2):
        tap = taps - 1 - row_tap if flip else row_tap
        items["repeat", flip] = (
            np.arange(taps * ins)[None, :] == (tap * ins + row_part)[:, None]
        )
    for dx in range(3):
        items["band", dx] = lane_slice[None, :] == row_slice[:, None] + dx - 1
    names = ("ahead", "ahead_low", "back", "back_low", "down", "down_low")
    items.update(zip(names, fourier_tables(height, depth)))
    lanes = -(-max(item.shape[1] for item in items.values()) // 128) * 128
    places, blocks, at = {}, [], 0
    for name, item in items.items():
        count = -(-item.shape[0] // 16) * 16
        block = np.zeros((count, lanes), jnp.bfloat16)
        block[: item.shape[0], : item.shape[1]] = np.asarray(item).astype(jnp.bfloat16)
        places[name] = (at, item.shape)
        blocks.append(block)
        at += count
    return np.concatenate(blocks), places


def dot(left, right):
    return jnp.dot(left, right, preferred_element_type=f32)


def dot_nt(left, right):
    return lax.dot_general(left, right, (((1,), (1,)), ((), ())), preferred_element_type=f32)


def halves(values):
    high = values.astype(bf16)
    return high, (values - high.astype(f32)).astype(bf16)


def spectrum(images, get, inverse, fine):
    count, height, depth = len(images), images[0].shape[0], images[0].shape[1] // 2
    names = ("back", "back_low") if inverse else ("ahead", "ahead_low")
    high, low = halves(jnp.concatenate(images, axis=0))
    turned = dot(high, get(names[0]))
    if fine:
        turned = turned + dot(high, get(names[1]))
    turned = jnp.concatenate(
        [turned[at * height : (at + 1) * height] for at in range(count)], axis=1
    )
    high = turned.astype(bf16)
    both_parts = dot(get("down"), high)
    results = []
    for at in range(count):
        start = 2 * at * depth
        upper = both_parts[:height, start : start + 2 * depth]
        lower = both_parts[height:, start : start + 2 * depth]
        if inverse:
            results.append(
                (upper[:, :depth] - lower[:, depth:], lower[:, :depth] + upper[:, depth:])
            )
        else:
            results.append(
                (upper[:, :depth] + lower[:, depth:], upper[:, depth:] - lower[:, :depth])
            )
    return results


def normal_part(real, imag, maps, kspace, mask, get):
    images = []
    for coil in range(maps.shape[0]):
        map_real, map_imag = maps[coil, 0, 0], maps[coil, 1, 0]
        images.append(
            jnp.concatenate(
                [map_real * real - map_imag * imag, map_real * imag + map_imag * real], axis=1
            )
        )
    masked = []
    for coil, (freq_real, freq_imag) in enumerate(spectrum(images, get, False, False)):
        if kspace is not None:
            freq_real = freq_real - kspace[coil, 0, 0]
            freq_imag = freq_imag - kspace[coil, 1, 0]
        masked.append(jnp.concatenate([mask * freq_real, mask * freq_imag], axis=1))
    total = None
    for coil, (real, imag) in enumerate(spectrum(masked, get, True, kspace is not None)):
        map_real, map_imag = maps[coil, 0, 0], maps[coil, 1, 0]
        term = (map_real * real + map_imag * imag, map_real * imag - map_imag * real)
        total = term if total is None else (total[0] + term[0], total[1] + term[1])
    return total


def build_in(flat, flip, get, target, slices):
    outs = flat.shape[2]
    lane = lax.broadcasted_iota(jnp.int32, (outs, target.shape[1]), 1).astype(f32)
    ins = target.shape[1] // (9 * slices)
    lane_slice = jnp.floor((lane + 0.5) * (1.0 / ins))
    lane_slice = lane_slice - slices * jnp.floor((lane_slice + 0.5) * (1.0 / slices))
    wide = []
    for dx in range(3):
        turned = dot_nt(get("eye"), flat[2 - dx if flip else dx].astype(bf16)).astype(bf16)
        wide.append(dot(turned, get("spread")))
    for out_slice in range(slices):
        block = None
        for dx in range(3):
            term = jnp.where(lane_slice == float(out_slice + dx - 1), wide[dx], 0.0)
            block = term if block is None else block + term
        target[out_slice * outs : (out_slice + 1) * outs] = block.astype(bf16)


def build_out(flat, flip, get, target):
    total = None
    for dx in range(3):
        wide = dot(flat[2 - dx if flip else dx].astype(bf16), get("tile")).astype(bf16)
        term = dot(get(("repeat", flip)), wide) * get(("band", dx)).astype(f32)
        total = term if total is None else total + term
    target[...] = total.astype(bf16)


def build_mid(raw, flip, get, target, slices):
    outs = raw.shape[3]
    hidden = outs * slices
    out_count, starts, width = groups_of(slices, hidden)
    blocks = []
    for dx in range(3):
        for dy in range(3):
            for dz in range(3):
                if flip:
                    blocks.append(dot_nt(get("eye"), raw[2 - dx, 2 - dy, 2 - dz]))
                else:
                    blocks.append(raw[dx, dy, dz].astype(f32))
    stacked = jnp.concatenate(blocks, axis=0).astype(bf16)
    for index, start in enumerate(starts):
        wide = dot(stacked, get(("mid", index)))
        lane = lax.broadcasted_iota(jnp.int32, (outs, width), 1).astype(f32) + float(start)
        lane_slice = jnp.floor((lane + 0.5) * (1.0 / outs))
        for out_at in range(out_count):
            out_slice = index * out_count + out_at
            keeps = [lane_slice == float(out_slice + dx - 1) for dx in range(3)]
            for tap in range(9):
                block = None
                for dx in range(3):
                    at = (dx * 9 + tap) * outs
                    term = jnp.where(keeps[dx], wide[at : at + outs], 0.0)
                    block = term if block is None else block + term
                at = (tap % 3 * out_count + out_at) * outs
                target[
                    index, at : at + outs, tap // 3 * width : (tap // 3 + 1) * width
                ] = block.astype(bf16)


def shifted(values, tap, depth):
    if tap == 1:
        return values
    lane = lax.broadcasted_iota(jnp.int32, (values.shape[0], depth), 1)
    edge, turn = (0, 1) if tap == 0 else (depth - 1, depth - 1)
    pieces = []
    for start in range(0, values.shape[1], depth):
        turned = pltpu.roll(values[:, start : start + depth], turn, 1)
        pieces.append(jnp.where(lane == edge, 0.0, turned))
    return jnp.concatenate(pieces, axis=1)


def conv_in(values, weights, depth):
    width = values.shape[1] - 2 * depth
    turned = [shifted(values, tap, depth) for tap in range(3)]
    stacked = jnp.concatenate(
        [turned[dz][:, dy * depth : dy * depth + width] for dy in range(3) for dz in range(3)],
        axis=0,
    )
    return dot(weights[...], stacked.astype(bf16))


def conv_mid(values, weights, depth, slices):
    cols = values.shape[1] - 2 * depth
    _, starts, width = groups_of(slices, values.shape[0])
    held = values.astype(bf16)
    totals = []
    for index, start in enumerate(starts):
        stacked = jnp.concatenate(
            [held[start : start + width, dy * depth : dy * depth + cols] for dy in range(3)],
            axis=0,
        )
        products = dot(weights[index], stacked)
        rows = products.shape[0] // 3
        total = products[rows : 2 * rows]
        for dz in (0, 2):
            total = total + shifted(products[dz * rows : (dz + 1) * rows], dz, depth)
        totals.append(total)
    return jnp.concatenate(totals, axis=0)


def conv_out(values, weights, depth):
    width = values.shape[1] - 2 * depth
    rows = weights.shape[0] // 9
    products = dot(weights[...], values.astype(bf16))
    total = None
    for dz in range(3):
        summed = None
        for dy in range(3):
            at = (dy * 3 + dz) * rows
            term = products[at : at + rows, dy * depth : dy * depth + width]
            summed = term if summed is None else summed + term
        term = shifted(summed, dz, depth)
        total = term if total is None else total + term
    return total


def sigmoid(values):
    return 0.5 + 0.5 * jnp.tanh(0.5 * values)


def step_kernel(places, *refs):
    (maps_in, kspace_in, mask_in, iterate_in, bits_in, adjoint_in, first_in, second_in,
     last_in, table_in, result, *refs) = refs
    (maps, kspace, mask, iterate, bits, adjoint, raw_first, raw_second, raw_last, table,
     load_sem, *refs) = refs
    (padded, padded_iterate, padded_fields, padded_relaxed, flats, work, rows_work,
     own_iterate, own_fields, all_iterate, halo, parts_send, parts, window_send, windows,
     fields_send, fields, delta_send, delta, grads_send, grads_back, own_pulled, all_pulled,
     sums_send, sums, first, second, last, first_t, second_t, last_t, exact, halo_sem, back_send,
     back_recv, pulled_send, pulled_recv, *sems) = refs
    channels = []
    for index, (axis, how, source, target) in enumerate((
        ("coil", "all", own_iterate, all_iterate),
        ("slab", "row", fields_send, fields),
        ("coil", "row", parts_send, parts),
        ("slab", "row", window_send, windows),
        ("slab", "row", delta_send, delta),
        ("coil", "row", sums_send.at[0], sums.at[0]),
        ("coil", "row", sums_send.at[1], sums.at[1]),
    )):
        channels.append(Channel(axis, how, source, target, sems[2 * index], sems[2 * index + 1]))
    (iterate_way, field_way, part_way, window_way, delta_way, *later) = channels
    sum_ways = later

    height, depth = mask.shape
    coils, _, rows, _ = all_iterate.shape
    slices, _, window, _ = windows.shape
    own = window - 2 * reach
    block = rows + 2 * reach
    my_coil, my_slab = lax.axis_index("coil"), lax.axis_index("slab")
    row_base = (my_coil * slices + my_slab) * own - reach
    coil_base = pl.multiple_of(my_coil * rows, 8)

    def get(name):
        at, shape = places[name]
        return table[at : at + shape[0], 0 : shape[1]]

    loads = {}
    tables_at = places["ahead"][0]
    for index, (name, source, target) in enumerate((
        ("iterate", iterate_in, iterate),
        ("bits", bits_in, bits),
        ("adjoint", adjoint_in, adjoint),
        ("second", second_in, raw_second),
        ("first", first_in, raw_first),
        ("last", last_in, raw_last),
        ("small", table_in.at[0:tables_at], table.at[0:tables_at]),
        ("maps", maps_in, maps),
        ("tables", table_in.at[tables_at:], table.at[tables_at:]),
        ("mask", mask_in, mask),
        ("kspace", kspace_in, kspace),
    )):
        loads[name] = pltpu.make_async_copy(source, target, load_sem.at[index])
    barrier, arrivals = greet()
    for load in loads.values():
        load.start()
    edge = jnp.zeros((2, 8, depth), f32)
    for target in (padded, padded_iterate):
        target[:, 0:8] = edge
        target[:, height + reach : height + reach + 8] = edge
    loads["iterate"].wait()
    own_iterate[...] = iterate[:, 0].astype(bf16)
    pl.semaphore_wait(barrier, arrivals)
    iterate_way.start()
    loads["bits"].wait()
    loads["adjoint"].wait()
    own_fields[0:2] = (2 * bits[:, 0] - 1).astype(bf16)
    own_fields[2:4] = adjoint[:, 0].astype(bf16)
    halo_ways = []
    for side, (turn, at) in enumerate(((1, rows - 8), (coils - 1, 0))):
        halo_ways.append(
            pltpu.make_async_remote_copy(
                src_ref=own_fields.at[:, at : at + 8],
                dst_ref=halo.at[side],
                send_sem=halo_sem.at[side],
                recv_sem=halo_sem.at[2 + side],
                device_id=place_of("coil", lax.rem(my_coil + turn, coils)),
                device_id_type=MESH,
            )
        )
        halo_ways[-1].start()
    for name in ("second", "first", "last", "small"):
        loads[name].wait()
    for side, raw in enumerate((raw_first, raw_last)):
        for dx in range(3):
            for tap in range(9):
                parts_of = raw[dx, tap // 3, tap % 3].astype(f32)
                flats[2 * side, dx, 2 * tap : 2 * tap + 2] = parts_of
                flats[2 * side + 1, dx, 16 - 2 * tap : 18 - 2 * tap] = parts_of
    build_in(flats.at[3], 1, get, last_t, slices)
    build_in(flats.at[0], 0, get, first, slices)
    build_mid(raw_second, 0, get, second, slices)
    build_mid(raw_second, 1, get, second_t, slices)
    for name in ("maps", "tables", "mask", "kspace"):
        loads[name].wait()
    weight = mask[...].astype(f32)
    all_iterate[my_coil] = own_iterate[...]
    iterate_way.finish()

    def column(gathered, channel):
        return jnp.concatenate(
            [gathered[piece, channel].astype(f32) for piece in range(coils)], axis=0
        )

    real, imag = column(all_iterate, 0), column(all_iterate, 1)
    total = normal_part(real, imag, maps, kspace, weight, get)
    padded[0, reach : reach + height] = total[0]
    padded[1, reach : reach + height] = total[1]
    for piece in range(coils):
        parts_send[piece] = padded[:, piece * rows : piece * rows + block].astype(bf16)
    part_way.start()
    padded_fields[:, reach : reach + rows] = own_fields[...].astype(f32)
    for way in halo_ways:
        way.wait()
    keep = jnp.where(my_coil > 0, 1.0, 0.0).astype(f32)
    padded_fields[:, 0:reach] = halo[0, :, 8 - reach : 8].astype(f32) * keep
    keep = jnp.where(my_coil < coils - 1, 1.0, 0.0).astype(f32)
    padded_fields[:, reach + rows : block] = halo[1, :, 0:reach].astype(f32) * keep
    for piece in range(slices):
        fields_send[piece] = padded_fields[:, piece * own : piece * own + window].astype(bf16)
    field_way.start()
    padded_iterate[0, reach : reach + height] = real
    padded_iterate[1, reach : reach + height] = imag
    padded_relaxed[:, 0:block] = padded_iterate[:, pl.ds(coil_base, block)]
    padded_relaxed[:, reach : reach + rows] = iterate[:, 0]

    def load(values):
        work[...] = values.astype(f32).reshape(work.shape)
        return jnp.concatenate([work[:, row, :] for row in range(window)], axis=1)

    def cut(values, before, after):
        return values[:, before * depth : values.shape[1] - after * depth]

    def inside(values, offset):
        blocks = []
        for row in range(values.shape[1] // depth):
            at = row_base + offset + row
            keep = jnp.where((at >= 0) & (at < height), 1.0, 0.0).astype(f32)
            blocks.append(values[:, row * depth : (row + 1) * depth] * keep)
        return jnp.concatenate(blocks, axis=1)

    def store(values):
        for row in range(own):
            rows_work[:, row, :] = values[:, row * depth : (row + 1) * depth]
        return rows_work[...].reshape(slices, 2, own, depth).astype(bf16)

    build_out(flats.at[2], 0, get, last)
    build_out(flats.at[0], 1, get, first_t)
    part_way.finish()
    summed = padded[:, pl.ds(coil_base, block)]
    for step in range(1, coils):
        summed = summed + parts[lax.rem(my_coil + step, coils)].astype(f32)
    padded_relaxed[:, 0:block] = padded_relaxed[:, 0:block] - step_size * summed
    for piece in range(slices):
        window_send[piece] = padded_relaxed[:, piece * own : piece * own + window].astype(bf16)
    window_way.start()
    windows[my_slab] = window_send[my_slab]
    pair = 2 if slices % 2 == 0 else 1
    groups = slices // pair
    my_group = lax.div(my_slab, pair)

    def send_back(field):
        for step in far_first(slices):
            rank = lax.rem(my_slab + step, slices)
            group = lax.rem(my_group + groups - lax.div(rank, pair), groups)
            pltpu.make_async_remote_copy(
                src_ref=grads_send.at[field, rank],
                dst_ref=grads_back.at[field, my_slab],
                send_sem=back_send.at[field],
                recv_sem=back_recv.at[field, group],
                device_id=place_of("slab", rank),
                device_id_type=MESH,
            ).start()

    def pass_on(field):
        for step in range(groups):
            count = pair if step else pair - 1
            group = lax.rem(my_group + step, groups)
            if count:
                landed = grads_back.at[field, 0:count]
                pltpu.make_async_copy(landed, landed, back_recv.at[field, step]).wait()
            for index in range(pair):
                piece = group * pair + index
                own_pulled[field, piece] = (
                    exact[field, piece] + grads_back[field, piece].astype(f32)
                ).astype(bf16)
            span = pl.ds(group * pair, pair)
            for turn in range(1, coils):
                pltpu.make_async_remote_copy(
                    src_ref=own_pulled.at[field, span],
                    dst_ref=all_pulled.at[field, my_coil, span],
                    send_sem=pulled_send.at[field],
                    recv_sem=pulled_recv.at[field],
                    device_id=place_of("coil", lax.rem(my_coil + turn, coils)),
                    device_id_type=MESH,
                ).start()
        all_pulled[field, my_coil] = own_pulled[field]

    for piece in range(slices):
        at = slice(piece * own, (piece + 1) * own)
        exact[0, piece] = (2 * bits[:, 0, at] - 1).astype(f32)
        exact[1, piece] = adjoint[:, 0, at]
    fields[my_slab] = fields_send[my_slab]
    field_way.finish()
    grads = []
    for field in range(2):
        probe = cut(load(fields[:, 2 * field : 2 * field + 2]), 1, 1)
        grads.append(conv_in(probe, last_t, depth))
    window_way.finish()

    pre1 = conv_in(load(windows[...]), first, depth)
    sig1 = sigmoid(pre1)
    act1 = pre1 * sig1
    slope1 = inside(cut(sig1 + act1 * (1.0 - sig1), 2, 2), 3)
    act1 = inside(act1, 1)
    pre2 = conv_mid(act1, second, depth, slices)
    sig2 = sigmoid(pre2)
    act2 = pre2 * sig2
    slope2 = inside(sig2 + act2 * (1.0 - sig2), 2)
    for field in range(2):
        grad1 = conv_mid(grads[field] * slope2, second_t, depth, slices) * slope1
        grads_send[field] = store(conv_out(grad1, first_t, depth))
        send_back(field)
        grads_back[field, my_slab] = grads_send[field, my_slab]
    act2 = inside(cut(act2, 1, 1), 3)
    delta_out = store(conv_out(act2, last, depth))

    for field in range(2):
        pass_on(field)
        if field == 0:
            delta_send[...] = delta_out
            delta_way.start()
            delta[my_slab] = delta_send[my_slab]
    partial = []
    for field in range(2):
        landed = all_pulled.at[field, 0 : coils - 1]
        for sem in (pulled_send, pulled_recv):
            pltpu.make_async_copy(landed, landed, sem.at[field]).wait()
        real, imag = (
            jnp.concatenate(
                [
                    all_pulled[field, piece // slices, piece % slices, part].astype(f32)
                    for piece in range(coils * slices)
                ],
                axis=0,
            )
            for part in range(2)
        )
        total = normal_part(real, imag, maps, None, weight, get)
        for part in range(2):
            padded[part, 0:height] = total[part]
            for piece in range(coils):
                sums_send[field, piece, part] = total[part][
                    piece * rows : (piece + 1) * rows
                ].astype(bf16)
        sum_ways[field].start()
        partial.append(padded[:, pl.ds(coil_base, rows)])

    backs = []
    for field in range(2):
        landed = grads_back.at[field, 0 : slices - 1]
        pltpu.make_async_copy(landed, landed, back_send.at[field]).wait()
        backs.append(
            jnp.concatenate(
                [grads_back[field, piece].astype(f32) for piece in range(slices)], axis=1
            )
        )
    delta_way.finish()
    for piece in range(slices):
        at = piece * own
        result[0, :, at : at + own] = (
            padded_relaxed[:, reach + at : reach + at + own] - iterate[:, 0, at : at + own]
        ) + delta[piece].astype(f32)
    for field in range(2):
        sum_ways[field].finish()
        added = partial[field]
        for step in range(1, coils):
            added = added + sums[field, lax.rem(my_coil + step, coils)].astype(f32)
        result[1 + field] = backs[field] - step_size * added


def on_device(coil_maps, kspace, sample_mask, iterate, probe_bits, loss_gradient, adjoint,
              kernel_first, kernel_second, kernel_last):
    height, depth = sample_mask.shape
    coils, slabs = lax.axis_size("coil"), lax.axis_size("slab")
    own = height // (coils * slabs)
    window = own + 2 * reach
    rows = iterate.shape[2]
    block = rows + 2 * reach
    hidden, channels = kernel_second.shape[0] * slabs, kernel_first.shape[1] * slabs
    table, places = pack_constants(height, depth, slabs, hidden, channels)
    raws = (
        jnp.transpose(kernel_first, (2, 3, 4, 1, 0)),
        jnp.transpose(kernel_second, (2, 3, 4, 0, 1)),
        jnp.transpose(kernel_last, (2, 3, 4, 0, 1)),
    )
    operands = (coil_maps, kspace, sample_mask, iterate, probe_bits, adjoint, *raws,
                jnp.asarray(table))
    _, starts, width = groups_of(slabs, hidden)
    mids = (len(starts), 3 * hidden // len(starts), 3 * width)
    buffers = [
        ((2, height + 2 * reach + 8, depth), f32),
        ((2, height + 2 * reach + 8, depth), f32),
        ((4, block + 8, depth), f32),
        ((2, block + 8, depth), f32),
        ((4, 3, 18, kernel_second.shape[0]), f32),
        ((2 * slabs, window, depth), f32),
        ((2 * slabs, own, depth), f32),
        ((2, rows, depth), bf16),
        ((4, rows, depth), bf16),
        ((coils, 2, rows, depth), bf16),
        ((2, 4, 8, depth), bf16),
        ((coils, 2, block, depth), bf16),
        ((coils, 2, block, depth), bf16),
        ((slabs, 2, window, depth), bf16),
        ((slabs, 2, window, depth), bf16),
        ((slabs, 4, window, depth), bf16),
        ((slabs, 4, window, depth), bf16),
        ((slabs, 2, own, depth), bf16),
        ((slabs, 2, own, depth), bf16),
        ((2, slabs, 2, own, depth), bf16),
        ((2, slabs, 2, own, depth), bf16),
        ((2, slabs, 2, own, depth), bf16),
        ((2, coils, slabs, 2, own, depth), bf16),
        ((2, coils, 2, rows, depth), bf16),
        ((2, coils, 2, rows, depth), bf16),
        ((hidden, 9 * channels), bf16),
        (mids, bf16),
        ((9 * channels, hidden), bf16),
        ((9 * channels, hidden), bf16),
        (mids, bf16),
        ((hidden, 9 * channels), bf16),
        ((2, slabs, 2, own, depth), f32),
    ]
    groups = slabs // 2 if slabs % 2 == 0 else slabs
    changes = pl.pallas_call(
        lambda *refs: step_kernel(places, *refs),
        out_shape=pltpu.VMEM((3, 2, rows, depth), f32),
        in_specs=[in_hbm] * len(operands),
        out_specs=in_vmem,
        scratch_shapes=[pltpu.VMEM(value.shape, value.dtype) for value in operands]
        + [pltpu.SemaphoreType.DMA((11,))]
        + [pltpu.VMEM(shape, kind) for shape, kind in buffers]
        + [pltpu.SemaphoreType.DMA((4,))]
        + [pltpu.SemaphoreType.DMA((2,)), pltpu.SemaphoreType.DMA((2, groups))]
        + [pltpu.SemaphoreType.DMA((2,))] * 2
        + [pltpu.SemaphoreType.DMA] * 14,
        compiler_params=pltpu.CompilerParams(
            collective_id=0, has_side_effects=True, vmem_limit_bytes=40 << 20
        ),
        name="step",
    )(*[pltpu.with_memory_space_constraint(value, pltpu.HBM) for value in operands])
    changes = changes[:, :, None]
    sign = (2 * probe_bits - 1).astype(f32)
    return iterate + changes[0], sign + changes[1], loss_gradient + (adjoint + changes[2])


def solution(mesh):
    split_coils = P("coil", None, "slab", None, None)
    image = P(None, "slab", "coil", None)
    return jax.shard_map(
        on_device,
        mesh=mesh,
        in_specs=(split_coils, split_coils, P(), image, image, image, image, P(), P(), P()),
        out_specs=(image, image, image),
        check_vma=False,
    )
```

```python
import jax
import jax.numpy as jnp
import numpy as np
from jax import lax
from jax.experimental import pallas as pl
from jax.experimental.pallas import tpu as pltpu
from jax.sharding import PartitionSpec as P

step_size = 0.8
reach = 4
f32 = jnp.float32
bf16 = jnp.bfloat16
in_hbm = pl.BlockSpec(memory_space=pltpu.HBM)
in_vmem = pl.BlockSpec(memory_space=pltpu.VMEM)
MESH = pl.DeviceIdType.MESH


class Channel:
    def __init__(self, axis, how, source, target, send_sem, recv_sem):
        self.axis, self.how, self.source, self.target = axis, how, source, target
        self.send_sem, self.recv_sem = send_sem, recv_sem
        self.size, self.mine = lax.axis_size(axis), lax.axis_index(axis)

    def row(self, rank):
        return self.source if self.how == "all" else self.source.at[rank]

    def copy(self, source_rank, target_row, device_rank):
        return pltpu.make_async_remote_copy(
            src_ref=self.row(source_rank),
            dst_ref=self.target.at[target_row],
            send_sem=self.send_sem,
            recv_sem=self.recv_sem,
            device_id=place_of(self.axis, device_rank),
            device_id_type=MESH,
        )

    def start(self):
        for step in range(1, self.size):
            rank = lax.rem(self.mine + step, self.size)
            self.copy(rank, self.mine, rank).start()

    def finish(self):
        landed = self.target.at[0 : self.size - 1]
        for sem in (self.send_sem, self.recv_sem):
            pltpu.make_async_copy(landed, landed, sem).wait()


def place_of(axis, rank):
    if axis == "coil":
        return rank, lax.axis_index("slab")
    return lax.axis_index("coil"), rank


def greet():
    barrier = pltpu.get_barrier_semaphore()
    count = 0
    for axis in ("coil", "slab"):
        size = lax.axis_size(axis)
        for step in range(1, size):
            rank = lax.rem(lax.axis_index(axis) + step, size)
            pl.semaphore_signal(
                barrier, inc=1, device_id=place_of(axis, rank), device_id_type=MESH
            )
            count += 1
    return barrier, count


def high_low(table):
    high = np.asarray(table, np.float32).astype(jnp.bfloat16)
    return high, (np.asarray(table, np.float32) - high.astype(np.float32)).astype(jnp.bfloat16)


def fourier_tables(height, depth):
    def parts(length):
        counter = np.arange(length)
        angles = (counter[:, None] * counter[None, :] % length) * (2.0 * np.pi / length)
        return np.cos(angles) / np.sqrt(length), np.sin(angles) / np.sqrt(length)

    cos, sin = parts(depth)
    forward = np.block([[cos, -sin], [sin, cos]])
    backward = np.block([[cos, sin], [-sin, cos]])
    return high_low(forward) + high_low(backward) + high_low(np.concatenate(parts(height)))


def groups_of(slices, hidden):
    per = hidden // slices
    out = 4 if slices % 4 == 0 else slices
    spans = []
    for first in range(0, slices, out):
        low = max(first - 1, 0) * per // 32 * 32
        high = min(first + out + 1, slices) * per
        spans.append((low, high))
    width = -(-max(high - low for low, high in spans) // 128) * 128
    if width >= hidden:
        return slices, [0], hidden
    return out, [min(low, hidden - width) for low, _ in spans], width


def mid_eye(hidden, slices, start, width):
    lanes = start + np.arange(width)
    return np.arange(hidden // slices)[:, None] == lanes[None, :] % (hidden // slices)


def pack_constants(height, depth, slices, hidden, channels):
    outs, ins = hidden // slices, channels // slices
    _, starts, width = groups_of(slices, hidden)
    taps = 9
    rows = np.arange(taps * slices * ins)
    row_slice, row_part, row_tap = rows // ins % slices, rows % ins, rows // (slices * ins)
    lane_slice = np.arange(hidden) // outs
    items = {
        "eye": np.eye(outs),
        "spread": np.kron(np.eye(taps), np.tile(np.eye(ins), (1, slices))),
        "tile": np.tile(np.eye(outs), (1, slices)),
    }
    for index, start in enumerate(starts):
        items["mid", index] = mid_eye(hidden, slices, start, width)
    for flip in range(2):
        tap = taps - 1 - row_tap if flip else row_tap
        items["repeat", flip] = (
            np.arange(taps * ins)[None, :] == (tap * ins + row_part)[:, None]
        )
    for dx in range(3):
        items["band", dx] = lane_slice[None, :] == row_slice[:, None] + dx - 1
    names = ("ahead", "ahead_low", "back", "back_low", "down", "down_low")
    items.update(zip(names, fourier_tables(height, depth)))
    lanes = -(-max(item.shape[1] for item in items.values()) // 128) * 128
    places, blocks, at = {}, [], 0
    for name, item in items.items():
        count = -(-item.shape[0] // 16) * 16
        block = np.zeros((count, lanes), jnp.bfloat16)
        block[: item.shape[0], : item.shape[1]] = np.asarray(item).astype(jnp.bfloat16)
        places[name] = (at, item.shape)
        blocks.append(block)
        at += count
    return np.concatenate(blocks), places


def dot(left, right):
    return jnp.dot(left, right, preferred_element_type=f32)


def dot_nt(left, right):
    return lax.dot_general(left, right, (((1,), (1,)), ((), ())), preferred_element_type=f32)


def halves(values):
    high = values.astype(bf16)
    return high, (values - high.astype(f32)).astype(bf16)


def spectrum(images, get, inverse, fine):
    count, height, depth = len(images), images[0].shape[0], images[0].shape[1] // 2
    names = ("back", "back_low") if inverse else ("ahead", "ahead_low")
    high, low = halves(jnp.concatenate(images, axis=0))
    turned = dot(high, get(names[0]))
    if fine:
        turned = turned + (dot(low, get(names[0])) + dot(high, get(names[1])))
    turned = jnp.concatenate(
        [turned[at * height : (at + 1) * height] for at in range(count)], axis=1
    )
    high = turned.astype(bf16)
    both_parts = dot(get("down"), high)
    results = []
    for at in range(count):
        start = 2 * at * depth
        upper = both_parts[:height, start : start + 2 * depth]
        lower = both_parts[height:, start : start + 2 * depth]
        if inverse:
            results.append(
                (upper[:, :depth] - lower[:, depth:], lower[:, :depth] + upper[:, depth:])
            )
        else:
            results.append(
                (upper[:, :depth] + lower[:, depth:], upper[:, depth:] - lower[:, :depth])
            )
    return results


def normal_part(real, imag, maps, kspace, mask, get):
    images = []
    for coil in range(maps.shape[0]):
        map_real, map_imag = maps[coil, 0, 0], maps[coil, 1, 0]
        images.append(
            jnp.concatenate(
                [map_real * real - map_imag * imag, map_real * imag + map_imag * real], axis=1
            )
        )
    masked = []
    for coil, (freq_real, freq_imag) in enumerate(spectrum(images, get, False, False)):
        if kspace is not None:
            freq_real = freq_real - kspace[coil, 0, 0]
            freq_imag = freq_imag - kspace[coil, 1, 0]
        masked.append(jnp.concatenate([mask * freq_real, mask * freq_imag], axis=1))
    total = None
    for coil, (real, imag) in enumerate(spectrum(masked, get, True, kspace is not None)):
        map_real, map_imag = maps[coil, 0, 0], maps[coil, 1, 0]
        term = (map_real * real + map_imag * imag, map_real * imag - map_imag * real)
        total = term if total is None else (total[0] + term[0], total[1] + term[1])
    return total


def field_turned(real, imag, maps, mask, get):
    images = []
    for coil in range(maps.shape[0]):
        map_real, map_imag = maps[coil, 0, 0], maps[coil, 1, 0]
        images.append(
            jnp.concatenate(
                [map_real * real - map_imag * imag, map_real * imag + map_imag * real], axis=1
            )
        )
    masked = [
        jnp.concatenate([mask * freq_real, mask * freq_imag], axis=1).astype(bf16)
        for freq_real, freq_imag in spectrum(images, get, False, False)
    ]
    height = real.shape[0]
    turned = dot(jnp.concatenate(masked, axis=0), get("back")).astype(bf16)
    return jnp.concatenate(
        [turned[at * height : (at + 1) * height] for at in range(len(masked))], axis=1
    )


def build_in(flat, flip, get, target, slices):
    outs = flat.shape[2]
    lane = lax.broadcasted_iota(jnp.int32, (outs, target.shape[1]), 1).astype(f32)
    ins = target.shape[1] // (9 * slices)
    lane_slice = jnp.floor((lane + 0.5) * (1.0 / ins))
    lane_slice = lane_slice - slices * jnp.floor((lane_slice + 0.5) * (1.0 / slices))
    wide = []
    for dx in range(3):
        turned = dot_nt(get("eye"), flat[2 - dx if flip else dx].astype(bf16)).astype(bf16)
        wide.append(dot(turned, get("spread")))
    for out_slice in range(slices):
        block = None
        for dx in range(3):
            term = jnp.where(lane_slice == float(out_slice + dx - 1), wide[dx], 0.0)
            block = term if block is None else block + term
        target[out_slice * outs : (out_slice + 1) * outs] = block.astype(bf16)


def build_out(flat, flip, get, target):
    total = None
    for dx in range(3):
        wide = dot(flat[2 - dx if flip else dx].astype(bf16), get("tile")).astype(bf16)
        term = dot(get(("repeat", flip)), wide) * get(("band", dx)).astype(f32)
        total = term if total is None else total + term
    target[...] = total.astype(bf16)


def build_mid(raw, flip, get, target, slices):
    outs = raw.shape[3]
    hidden = outs * slices
    out_count, starts, width = groups_of(slices, hidden)
    blocks = []
    for dx in range(3):
        for dy in range(3):
            for dz in range(3):
                if flip:
                    blocks.append(dot_nt(get("eye"), raw[2 - dx, 2 - dy, 2 - dz]))
                else:
                    blocks.append(raw[dx, dy, dz].astype(f32))
    stacked = jnp.concatenate(blocks, axis=0).astype(bf16)
    for index, start in enumerate(starts):
        wide = dot(stacked, get(("mid", index)))
        lane = lax.broadcasted_iota(jnp.int32, (outs, width), 1).astype(f32) + float(start)
        lane_slice = jnp.floor((lane + 0.5) * (1.0 / outs))
        for out_at in range(out_count):
            out_slice = index * out_count + out_at
            keeps = [lane_slice == float(out_slice + dx - 1) for dx in range(3)]
            for tap in range(9):
                block = None
                for dx in range(3):
                    at = (dx * 9 + tap) * outs
                    term = jnp.where(keeps[dx], wide[at : at + outs], 0.0)
                    block = term if block is None else block + term
                at = (tap % 3 * out_count + out_at) * outs
                target[
                    index, at : at + outs, tap // 3 * width : (tap // 3 + 1) * width
                ] = block.astype(bf16)


def shifted(values, tap, depth):
    if tap == 1:
        return values
    lane = lax.broadcasted_iota(jnp.int32, (values.shape[0], depth), 1)
    edge, turn = (0, 1) if tap == 0 else (depth - 1, depth - 1)
    pieces = []
    for start in range(0, values.shape[1], depth):
        turned = pltpu.roll(values[:, start : start + depth], turn, 1)
        pieces.append(jnp.where(lane == edge, 0.0, turned))
    return jnp.concatenate(pieces, axis=1)


def conv_in(values, weights, depth):
    width = values.shape[1] - 2 * depth
    turned = [shifted(values, tap, depth) for tap in range(3)]
    stacked = jnp.concatenate(
        [turned[dz][:, dy * depth : dy * depth + width] for dy in range(3) for dz in range(3)],
        axis=0,
    )
    return dot(weights[...], stacked.astype(bf16))


def conv_mid(values, weights, depth, slices):
    cols = values.shape[1] - 2 * depth
    _, starts, width = groups_of(slices, values.shape[0])
    held = values.astype(bf16)
    totals = []
    for index, start in enumerate(starts):
        stacked = jnp.concatenate(
            [held[start : start + width, dy * depth : dy * depth + cols] for dy in range(3)],
            axis=0,
        )
        products = dot(weights[index], stacked)
        rows = products.shape[0] // 3
        total = products[rows : 2 * rows]
        for dz in (0, 2):
            total = total + shifted(products[dz * rows : (dz + 1) * rows], dz, depth)
        totals.append(total)
    return jnp.concatenate(totals, axis=0)


def conv_out(values, weights, depth):
    width = values.shape[1] - 2 * depth
    rows = weights.shape[0] // 9
    products = dot(weights[...], values.astype(bf16))
    total = None
    for dz in range(3):
        summed = None
        for dy in range(3):
            at = (dy * 3 + dz) * rows
            term = products[at : at + rows, dy * depth : dy * depth + width]
            summed = term if summed is None else summed + term
        term = shifted(summed, dz, depth)
        total = term if total is None else total + term
    return total


def sigmoid(values):
    return 0.5 + 0.5 * jnp.tanh(0.5 * values)


def step_kernel(places, *refs):
    (maps_in, kspace_in, mask_in, iterate_in, bits_in, adjoint_in, first_in, second_in,
     last_in, table_in, result, *refs) = refs
    (maps, kspace, mask, iterate, bits, adjoint, raw_first, raw_second, raw_last, table,
     load_sem, *refs) = refs
    (padded, padded_iterate, padded_fields, padded_relaxed, flats, work, rows_work,
     own_iterate, own_fields, all_iterate, halo, parts_send, parts, window_send, windows,
     fields_send, fields, delta_send, delta, grads_send, grads_back, own_pulled, all_pulled,
     sums_send, sums, first, second, last, first_t, second_t, last_t, exact, halo_sem, back_send,
     back_recv, pulled_send, pulled_recv, *sems) = refs
    channels = []
    for index, (axis, how, source, target) in enumerate((
        ("coil", "all", own_iterate, all_iterate),
        ("slab", "row", fields_send, fields),
        ("coil", "row", parts_send, parts),
        ("slab", "row", window_send, windows),
        ("slab", "row", delta_send, delta),
        ("coil", "row", sums_send.at[0], sums.at[0]),
        ("coil", "row", sums_send.at[1], sums.at[1]),
    )):
        channels.append(Channel(axis, how, source, target, sems[2 * index], sems[2 * index + 1]))
    (iterate_way, field_way, part_way, window_way, delta_way, *later) = channels
    sum_ways = later

    height, depth = mask.shape
    coils, _, rows, _ = all_iterate.shape
    slices, _, window, _ = windows.shape
    own = window - 2 * reach
    block = rows + 2 * reach
    my_coil, my_slab = lax.axis_index("coil"), lax.axis_index("slab")
    row_base = (my_coil * slices + my_slab) * own - reach
    coil_base = pl.multiple_of(my_coil * rows, 8)

    def get(name):
        at, shape = places[name]
        return table[at : at + shape[0], 0 : shape[1]]

    loads = {}
    tables_at = places["ahead"][0]
    for index, (name, source, target) in enumerate((
        ("iterate", iterate_in, iterate),
        ("bits", bits_in, bits),
        ("adjoint", adjoint_in, adjoint),
        ("second", second_in, raw_second),
        ("first", first_in, raw_first),
        ("last", last_in, raw_last),
        ("small", table_in.at[0:tables_at], table.at[0:tables_at]),
        ("maps", maps_in, maps),
        ("tables", table_in.at[tables_at:], table.at[tables_at:]),
        ("mask", mask_in, mask),
        ("kspace", kspace_in, kspace),
    )):
        loads[name] = pltpu.make_async_copy(source, target, load_sem.at[index])
    barrier, arrivals = greet()
    for load in loads.values():
        load.start()
    edge = jnp.zeros((2, 8, depth), f32)
    for target in (padded, padded_iterate):
        target[:, 0:8] = edge
        target[:, height + reach : height + reach + 8] = edge
    loads["iterate"].wait()
    own_iterate[...] = iterate[:, 0].astype(bf16)
    pl.semaphore_wait(barrier, arrivals)
    iterate_way.start()
    loads["bits"].wait()
    loads["adjoint"].wait()
    own_fields[0:2] = (2 * bits[:, 0] - 1).astype(bf16)
    own_fields[2:4] = adjoint[:, 0].astype(bf16)
    halo_ways = []
    for side, (turn, at) in enumerate(((1, rows - 8), (coils - 1, 0))):
        halo_ways.append(
            pltpu.make_async_remote_copy(
                src_ref=own_fields.at[:, at : at + 8],
                dst_ref=halo.at[side],
                send_sem=halo_sem.at[side],
                recv_sem=halo_sem.at[2 + side],
                device_id=place_of("coil", lax.rem(my_coil + turn, coils)),
                device_id_type=MESH,
            )
        )
        halo_ways[-1].start()
    for name in ("second", "first", "last", "small"):
        loads[name].wait()
    for side, raw in enumerate((raw_first, raw_last)):
        for dx in range(3):
            for tap in range(9):
                parts_of = raw[dx, tap // 3, tap % 3].astype(f32)
                flats[2 * side, dx, 2 * tap : 2 * tap + 2] = parts_of
                flats[2 * side + 1, dx, 16 - 2 * tap : 18 - 2 * tap] = parts_of
    build_in(flats.at[3], 1, get, last_t, slices)
    build_in(flats.at[0], 0, get, first, slices)
    build_mid(raw_second, 0, get, second, slices)
    build_mid(raw_second, 1, get, second_t, slices)
    for name in ("maps", "tables", "mask", "kspace"):
        loads[name].wait()
    weight = mask[...].astype(f32)
    all_iterate[my_coil] = own_iterate[...]
    iterate_way.finish()

    def column(gathered, channel):
        return jnp.concatenate(
            [gathered[piece, channel].astype(f32) for piece in range(coils)], axis=0
        )

    real, imag = column(all_iterate, 0), column(all_iterate, 1)
    total = normal_part(real, imag, maps, kspace, weight, get)
    padded[0, reach : reach + height] = total[0]
    padded[1, reach : reach + height] = total[1]
    for piece in range(coils):
        parts_send[piece] = padded[:, piece * rows : piece * rows + block].astype(bf16)
    part_way.start()
    padded_fields[:, reach : reach + rows] = own_fields[...].astype(f32)
    for way in halo_ways:
        way.wait()
    keep = jnp.where(my_coil > 0, 1.0, 0.0).astype(f32)
    padded_fields[:, 0:reach] = halo[0, :, 8 - reach : 8].astype(f32) * keep
    keep = jnp.where(my_coil < coils - 1, 1.0, 0.0).astype(f32)
    padded_fields[:, reach + rows : block] = halo[1, :, 0:reach].astype(f32) * keep
    for piece in range(slices):
        fields_send[piece] = padded_fields[:, piece * own : piece * own + window].astype(bf16)
    field_way.start()
    padded_iterate[0, reach : reach + height] = real
    padded_iterate[1, reach : reach + height] = imag
    padded_relaxed[:, 0:block] = padded_iterate[:, pl.ds(coil_base, block)]
    padded_relaxed[:, reach : reach + rows] = iterate[:, 0]

    def load(values):
        work[...] = values.astype(f32).reshape(work.shape)
        return jnp.concatenate([work[:, row, :] for row in range(window)], axis=1)

    def cut(values, before, after):
        return values[:, before * depth : values.shape[1] - after * depth]

    def inside(values, offset):
        blocks = []
        for row in range(values.shape[1] // depth):
            at = row_base + offset + row
            keep = jnp.where((at >= 0) & (at < height), 1.0, 0.0).astype(f32)
            blocks.append(values[:, row * depth : (row + 1) * depth] * keep)
        return jnp.concatenate(blocks, axis=1)

    def store(values):
        for row in range(own):
            rows_work[:, row, :] = values[:, row * depth : (row + 1) * depth]
        return rows_work[...].reshape(slices, 2, own, depth).astype(bf16)

    build_out(flats.at[2], 0, get, last)
    build_out(flats.at[0], 1, get, first_t)
    part_way.finish()
    summed = padded[:, pl.ds(coil_base, block)]
    for step in range(1, coils):
        summed = summed + parts[lax.rem(my_coil + step, coils)].astype(f32)
    padded_relaxed[:, 0:block] = padded_relaxed[:, 0:block] - step_size * summed
    for piece in range(slices):
        window_send[piece] = padded_relaxed[:, piece * own : piece * own + window].astype(bf16)
    window_way.start()
    windows[my_slab] = window_send[my_slab]
    pair = 2 if slices % 2 == 0 else 1
    groups = slices // pair
    my_group = lax.div(my_slab, pair)

    def send_back(field):
        for step in range(1, slices):
            rank = lax.rem(my_slab + step, slices)
            group = lax.rem(my_group + groups - lax.div(rank, pair), groups)
            pltpu.make_async_remote_copy(
                src_ref=grads_send.at[field, rank],
                dst_ref=grads_back.at[field, my_slab],
                send_sem=back_send.at[field],
                recv_sem=back_recv.at[field, group],
                device_id=place_of("slab", rank),
                device_id_type=MESH,
            ).start()

    def pass_on(field):
        for step in range(groups):
            count = pair if step else pair - 1
            group = lax.rem(my_group + step, groups)
            if count:
                landed = grads_back.at[field, 0:count]
                pltpu.make_async_copy(landed, landed, back_recv.at[field, step]).wait()
            for index in range(pair):
                piece = group * pair + index
                own_pulled[field, piece] = (
                    exact[field, piece] + grads_back[field, piece].astype(f32)
                ).astype(bf16)
            span = pl.ds(group * pair, pair)
            for turn in range(1, coils):
                pltpu.make_async_remote_copy(
                    src_ref=own_pulled.at[field, span],
                    dst_ref=all_pulled.at[field, my_coil, span],
                    send_sem=pulled_send.at[field],
                    recv_sem=pulled_recv.at[field],
                    device_id=place_of("coil", lax.rem(my_coil + turn, coils)),
                    device_id_type=MESH,
                ).start()
        all_pulled[field, my_coil] = own_pulled[field]

    for piece in range(slices):
        at = slice(piece * own, (piece + 1) * own)
        exact[0, piece] = (2 * bits[:, 0, at] - 1).astype(f32)
        exact[1, piece] = adjoint[:, 0, at]
    fields[my_slab] = fields_send[my_slab]
    field_way.finish()
    grads = []
    for field in range(2):
        probe = cut(load(fields[:, 2 * field : 2 * field + 2]), 1, 1)
        grads.append(conv_in(probe, last_t, depth))
    window_way.finish()

    pre1 = conv_in(load(windows[...]), first, depth)
    sig1 = sigmoid(pre1)
    act1 = pre1 * sig1
    slope1 = inside(cut(sig1 + act1 * (1.0 - sig1), 2, 2), 3)
    act1 = inside(act1, 1)
    pre2 = conv_mid(act1, second, depth, slices)
    sig2 = sigmoid(pre2)
    act2 = pre2 * sig2
    slope2 = inside(sig2 + act2 * (1.0 - sig2), 2)
    for field in range(2):
        grad1 = conv_mid(grads[field] * slope2, second_t, depth, slices) * slope1
        grads_send[field] = store(conv_out(grad1, first_t, depth))
        send_back(field)
        grads_back[field, my_slab] = grads_send[field, my_slab]
    act2 = inside(cut(act2, 1, 1), 3)
    delta_out = store(conv_out(act2, last, depth))

    for field in range(2):
        pass_on(field)
        if field == 0:
            delta_send[...] = delta_out
            delta_way.start()
            delta[my_slab] = delta_send[my_slab]
    partial = []
    for field in range(2):
        landed = all_pulled.at[field, 0 : coils - 1]
        for sem in (pulled_send, pulled_recv):
            pltpu.make_async_copy(landed, landed, sem.at[field]).wait()
        real, imag = (
            jnp.concatenate(
                [
                    all_pulled[field, piece // slices, piece % slices, part].astype(f32)
                    for piece in range(coils * slices)
                ],
                axis=0,
            )
            for part in range(2)
        )
        turned = field_turned(real, imag, maps, weight, get)
        down_at = places["down"][0]
        for step in (*range(1, coils), 0):
            rank = lax.rem(my_coil + step, coils)
            base = pl.multiple_of(rank * rows, 8)
            left = jnp.concatenate(
                [
                    table[pl.ds(pl.multiple_of(down_at + part * height + base, 8), rows), 0:height]
                    for part in range(2)
                ],
                axis=0,
            )
            products = dot(left, turned)
            total = None
            for coil in range(maps.shape[0]):
                start = 2 * coil * depth
                upper = products[:rows, start : start + 2 * depth]
                lower = products[rows:, start : start + 2 * depth]
                real = upper[:, :depth] - lower[:, depth:]
                imag = lower[:, :depth] + upper[:, depth:]
                map_real = maps[coil, 0, 0, pl.ds(base, rows)]
                map_imag = maps[coil, 1, 0, pl.ds(base, rows)]
                term = (map_real * real + map_imag * imag, map_real * imag - map_imag * real)
                total = term if total is None else (total[0] + term[0], total[1] + term[1])
            if step:
                for part in range(2):
                    sums_send[field, rank, part] = total[part].astype(bf16)
                sum_ways[field].copy(rank, my_coil, rank).start()
            else:
                partial.append(jnp.stack(total))

    backs = []
    for field in range(2):
        landed = grads_back.at[field, 0 : slices - 1]
        pltpu.make_async_copy(landed, landed, back_send.at[field]).wait()
        backs.append(
            jnp.concatenate(
                [grads_back[field, piece].astype(f32) for piece in range(slices)], axis=1
            )
        )
    delta_way.finish()
    for piece in range(slices):
        at = piece * own
        result[0, :, at : at + own] = (
            padded_relaxed[:, reach + at : reach + at + own] - iterate[:, 0, at : at + own]
        ) + delta[piece].astype(f32)
    for field in range(2):
        sum_ways[field].finish()
        added = partial[field]
        for step in range(1, coils):
            added = added + sums[field, lax.rem(my_coil + step, coils)].astype(f32)
        result[1 + field] = backs[field] - step_size * added


def on_device(coil_maps, kspace, sample_mask, iterate, probe_bits, loss_gradient, adjoint,
              kernel_first, kernel_second, kernel_last):
    height, depth = sample_mask.shape
    coils, slabs = lax.axis_size("coil"), lax.axis_size("slab")
    own = height // (coils * slabs)
    window = own + 2 * reach
    rows = iterate.shape[2]
    block = rows + 2 * reach
    hidden, channels = kernel_second.shape[0] * slabs, kernel_first.shape[1] * slabs
    table, places = pack_constants(height, depth, slabs, hidden, channels)
    raws = (
        jnp.transpose(kernel_first, (2, 3, 4, 1, 0)),
        jnp.transpose(kernel_second, (2, 3, 4, 0, 1)),
        jnp.transpose(kernel_last, (2, 3, 4, 0, 1)),
    )
    operands = (coil_maps, kspace, sample_mask, iterate, probe_bits, adjoint, *raws,
                jnp.asarray(table))
    _, starts, width = groups_of(slabs, hidden)
    mids = (len(starts), 3 * hidden // len(starts), 3 * width)
    buffers = [
        ((2, height + 2 * reach + 8, depth), f32),
        ((2, height + 2 * reach + 8, depth), f32),
        ((4, block + 8, depth), f32),
        ((2, block + 8, depth), f32),
        ((4, 3, 18, kernel_second.shape[0]), f32),
        ((2 * slabs, window, depth), f32),
        ((2 * slabs, own, depth), f32),
        ((2, rows, depth), bf16),
        ((4, rows, depth), bf16),
        ((coils, 2, rows, depth), bf16),
        ((2, 4, 8, depth), bf16),
        ((coils, 2, block, depth), bf16),
        ((coils, 2, block, depth), bf16),
        ((slabs, 2, window, depth), bf16),
        ((slabs, 2, window, depth), bf16),
        ((slabs, 4, window, depth), bf16),
        ((slabs, 4, window, depth), bf16),
        ((slabs, 2, own, depth), bf16),
        ((slabs, 2, own, depth), bf16),
        ((2, slabs, 2, own, depth), bf16),
        ((2, slabs, 2, own, depth), bf16),
        ((2, slabs, 2, own, depth), bf16),
        ((2, coils, slabs, 2, own, depth), bf16),
        ((2, coils, 2, rows, depth), bf16),
        ((2, coils, 2, rows, depth), bf16),
        ((hidden, 9 * channels), bf16),
        (mids, bf16),
        ((9 * channels, hidden), bf16),
        ((9 * channels, hidden), bf16),
        (mids, bf16),
        ((hidden, 9 * channels), bf16),
        ((2, slabs, 2, own, depth), f32),
    ]
    groups = slabs // 2 if slabs % 2 == 0 else slabs
    changes = pl.pallas_call(
        lambda *refs: step_kernel(places, *refs),
        out_shape=pltpu.VMEM((3, 2, rows, depth), f32),
        in_specs=[in_hbm] * len(operands),
        out_specs=in_vmem,
        scratch_shapes=[pltpu.VMEM(value.shape, value.dtype) for value in operands]
        + [pltpu.SemaphoreType.DMA((11,))]
        + [pltpu.VMEM(shape, kind) for shape, kind in buffers]
        + [pltpu.SemaphoreType.DMA((4,))]
        + [pltpu.SemaphoreType.DMA((2,)), pltpu.SemaphoreType.DMA((2, groups))]
        + [pltpu.SemaphoreType.DMA((2,))] * 2
        + [pltpu.SemaphoreType.DMA] * 14,
        compiler_params=pltpu.CompilerParams(
            collective_id=0, has_side_effects=True, vmem_limit_bytes=40 << 20
        ),
        name="step",
    )(*[pltpu.with_memory_space_constraint(value, pltpu.HBM) for value in operands])
    changes = changes[:, :, None]
    sign = (2 * probe_bits - 1).astype(f32)
    return iterate + changes[0], sign + changes[1], loss_gradient + (adjoint + changes[2])


def solution(mesh):
    split_coils = P("coil", None, "slab", None, None)
    image = P(None, "slab", "coil", None)
    return jax.shard_map(
        on_device,
        mesh=mesh,
        in_specs=(split_coils, split_coils, P(), image, image, image, image, P(), P(), P()),
        out_specs=(image, image, image),
        check_vma=False,
    )
```
